256 devices in a mesh: acct: 64 (over z, x, core), rep: 4 (over y).
Axes of the slice: x: 4, y: 4, z: 8, core: 2. Of those that a mesh axis runs over, the one named last changes fastest.
Arguments:
- memory: bfloat16 [128, 512, 512], P('rep', 'acct'), may hold values from -3 to 3
- src_dev: int32 [3, 2048, 1], replicated, may hold values from 0 to 63; in each aligned block of 32 rows (0 to 31, 32 to 63, ..., all dimensions but the last counted through in order) at most 2 rows name the same one
- src_local: int32 [3, 2048], replicated, may hold values from 0 to 7
- dst_local: int32 [3, 2048], P(None, 'acct'), may hold values from 0 to 7
- delta_t: float32 [3, 2048], P(None, 'acct'), may hold values from 0.1 to 30
- masks: int32 [3, 2048, 128, 128], P(None, 'acct', 'rep'), may hold values 0 or 1
- member: int32 [3, 128, 512], P(None, 'rep', 'acct'), may hold values 0 or 1
- w_msg1: bfloat16 [512, 512], replicated, may hold values from -0.25 to 0.25
- b_msg1: float32 [512], replicated, may hold values from -3 to 3
- omega: float32 [512], replicated, may hold values from 0.05 to 3
- w_msg2: bfloat16 [512, 512], replicated, may hold values from -0.25 to 0.25
- ln_gain: float32 [512], replicated, may hold values from 0.25 to 1.75
- w_in: bfloat16 [512, 1536], replicated, may hold values from -0.25 to 0.25
- w_hid: bfloat16 [512, 1536], replicated, may hold values from -0.25 to 0.25
- b_in: float32 [1536], replicated, may hold values from -3 to 3
- b_hid: float32 [1536], replicated, may hold values from -3 to 3
Outputs:
- new_memory: bfloat16 [128, 512, 512], P('rep', 'acct')
The draws below stay inside these ranges and needn't reach their ends.
Inputs may be any that keep to these rules, and one draw needn't show every extreme that they name: In each batch, among the 32 tiles of one index of acct (rows t of one aligned block), at most 2 have the same src_dev.
All inputs are finite; a program needn't handle non-finite values. No bound on the sum of `masks` or of `member` on one device may be relied on, other than what follows from the above.
Results may differ from the reference program's by a relative error of at most 0.009.
Values may be sent and summed in bfloat16 or wider, within the bound.
No kernel may reach another device: no remote copies, remote signals or barrier semaphores. Data moves between devices by JAX's collectives and lax.ppermute only.
A program may use at most 128 MiB of HBM per device.

```python
import math
import jax
import jax.numpy as jnp
import numpy as np
from jax import lax

D = 512
HID = 512
BLK = 128
NB = 3
BLK_DEV = 8
TIL_DEV = 32
CAP = 2
BLOCKS = 512
TILES_A = 2048
N_ACCT = 64


def set_ends(entries, stream_key, low, largest):
    place = [jax.random.randint(jax.random.fold_in(stream_key, axis), (), 0, length) for axis, length in enumerate(entries.shape)]
    longest = entries.shape.index(max(entries.shape))
    beside = place[:longest] + [(place[longest] + 1) % entries.shape[longest]] + place[longest + 1:]
    return entries.at[tuple(place)].set(low).at[tuple(beside)].set(largest)


def levels(own_key, dims, split, smallest, high):
    gain, own = 1.0, jax.random.fold_in(own_key, 6)
    for position, blocks in split:
        draws = jnp.exp(jax.random.uniform(jax.random.fold_in(own, position), (blocks,), jnp.float32, smallest / len(split), high / len(split)))
        gain = gain * jnp.repeat(draws, dims[position] // blocks).reshape([-1 if axis == position else 1 for axis in range(len(dims))])
    return gain


def shared_out(stream_key, own, number, rows, amount, top, limit, slope):
    order = jax.random.permutation(stream_key, amount)
    heavy_load, common = shares(amount, rows * top, limit, slope, True), shares(amount, rows * top, limit, slope, False)
    places = jnp.arange(amount)

    def named(lengths, turn):
        used = int((lengths > 0).sum())
        fixed = max(1, used // 4)
        shifted = fixed + (places - fixed + turn * (used - fixed)) % max(1, amount - fixed)
        return jnp.zeros((amount,), jnp.int32).at[order[jnp.where(places < fixed, places, shifted)]].set(jnp.asarray(lengths, jnp.int32))

    lengths = jnp.where(number % 4 == 0, named(heavy_load, number // 4), named(common, number - number // 4 - 1))
    mixed = jax.random.permutation(jax.random.fold_in(own, 3), amount)
    giver, taker = mixed[0:amount // 2 * 2:2], mixed[1:amount // 2 * 2:2]
    room = jnp.minimum(lengths[giver] - 1, limit - lengths[taker]) // 2
    room = jnp.where((giver == order[0]) | (taker == order[0]) | (lengths[taker] == 0), 0, jnp.maximum(room, 0))
    shifted = jax.random.randint(jax.random.fold_in(own, 4), (amount // 2,), 0, 1 << 20) % (room + 1)
    lengths = lengths.at[giver].add(-shifted).at[taker].add(shifted)
    labels = jnp.searchsorted(jnp.cumsum(lengths), jnp.arange(rows * top), side="right").astype(jnp.int32)
    table = labels.reshape(top, rows).T
    table = table[jax.random.permutation(jax.random.fold_in(own, 1), rows)]
    turn = jax.random.randint(jax.random.fold_in(own, 2), (rows, 1), 0, top)
    return jnp.take_along_axis(table, (jnp.arange(top)[None, :] + turn) % top, axis=1)


def shares(count, total, bound, lean, full):
    portions = [(1 << 20) // math.isqrt(rank ** lean) + 1 for rank in range(1, count + 1)]
    largest = bound if full else min(bound, max(-(-total // count), total * portions[0] // sum(portions)))
    least = 1 if total - largest >= count - 1 else 0
    counts, spare = [largest] + [least] * (count - 1), total - largest - least * (count - 1)
    while spare > 0:
        movable = [i for i in range(1, count) if counts[i] < largest] or [i for i in range(1, count) if counts[i] < bound]
        mass, remaining = sum([portions[i] for i in movable]), spare
        for i in movable:
            addition = min(bound - counts[i], max(1, remaining * portions[i] // mass), spare)
            counts[i] = counts[i] + addition
            spare = spare - addition
    return np.array(counts)


def normal_values(key, shape, scale, reach, cuts=(), kind=jnp.bfloat16):
    factor_of = levels(key, shape, cuts, -0.22, 0.18) if cuts else 1.0
    values = jax.random.normal(key, shape, jnp.float32) * scale * factor_of
    return jnp.minimum(jnp.maximum(values, -reach), reach).astype(kind)


def setup_inputs(seed: int = 0) -> dict:
    arg_keys = jax.random.split(jax.random.key(seed), 17)
    memory = normal_values(arg_keys[0], (BLK, BLOCKS, D), 0.5, 3.0, ((0, 4), (1, 64)))
    src_dev_keys = jax.random.split(jax.random.fold_in(arg_keys[1], 1), NB * TILES_A // TIL_DEV)
    src_dev_turns = jax.random.permutation(jax.random.fold_in(arg_keys[1], 3), NB * TILES_A // TIL_DEV)
    src_dev = jax.vmap(lambda own, number: shared_out(jax.random.fold_in(arg_keys[1], 2), own, number, TIL_DEV, N_ACCT, 1, CAP, 2))(src_dev_keys, src_dev_turns).reshape((NB, TILES_A, 1))
    src_local = set_ends(jax.random.randint(arg_keys[2], (NB, TILES_A), 0, BLK_DEV), jax.random.fold_in(arg_keys[2], 1), 0, BLK_DEV - 1).astype(jnp.int32)
    dst_local = set_ends(jax.random.randint(arg_keys[3], (NB, TILES_A), 0, BLK_DEV), jax.random.fold_in(arg_keys[3], 1), 0, BLK_DEV - 1).astype(jnp.int32)
    delta_t = jnp.clip(jnp.exp(math.log(30.0) - 5.7037825 * jax.random.uniform(arg_keys[4], (NB, TILES_A), jnp.float32) ** levels(arg_keys[4], (NB, TILES_A), ((1, 64),), -0.2, 0.2)), 0.1, 30.0)
    masks = set_ends((jax.random.randint(arg_keys[5], (NB, TILES_A, BLK, BLK), 0, 4) < 1).astype(jnp.int32), jax.random.fold_in(arg_keys[5], 1), 0, 1)
    member = set_ends((jax.random.randint(arg_keys[6], (NB, BLK, BLOCKS), 0, 3) < 2).astype(jnp.int32), jax.random.fold_in(arg_keys[6], 1), 0, 1)
    w_msg1 = normal_values(arg_keys[7], (D, HID), D ** -0.5, 0.25)
    b_msg1 = normal_values(arg_keys[8], (HID,), 0.5, 3.0, (), jnp.float32)
    omega = jnp.clip(jnp.exp(jax.random.uniform(arg_keys[9], (HID,), jnp.float32, math.log(0.05), math.log(3.0))), 0.05, 3.0)
    w_msg2 = normal_values(arg_keys[10], (HID, D), HID ** -0.5, 0.25)
    ln_gain = jnp.clip(1.0 + 0.15 * jax.random.normal(arg_keys[11], (D,), jnp.float32), 0.25, 1.75)
    w_in = normal_values(arg_keys[12], (D, 3 * D), D ** -0.5, 0.25)
    w_hid = normal_values(arg_keys[13], (D, 3 * D), D ** -0.5, 0.25)
    b_in = normal_values(arg_keys[14], (3 * D,), 0.5, 3.0, (), jnp.float32)
    b_hid = normal_values(arg_keys[15], (3 * D,), 0.5, 3.0, (), jnp.float32)
    return dict(memory=memory, src_dev=src_dev, src_local=src_local, dst_local=dst_local, delta_t=delta_t, masks=masks, member=member, w_msg1=w_msg1, b_msg1=b_msg1, omega=omega, w_msg2=w_msg2, ln_gain=ln_gain, w_in=w_in, w_hid=w_hid, b_in=b_in, b_hid=b_hid)


def batch_step(state, batch, src_dev, src_local, dst_local, delta_t, masks, member, w_msg1, b_msg1, omega, w_msg2, ln_gain, w_in, w_hid, b_in, b_hid):
    flat = state.reshape(BLK * BLOCKS, D)
    pre = jnp.dot(flat, w_msg1, preferred_element_type=jnp.float32).astype(jnp.bfloat16).reshape(BLK, BLOCKS, HID)
    source = (src_dev[batch, :, 0] * BLK_DEV + src_local[batch]).astype(jnp.int32).reshape(N_ACCT, TIL_DEV)
    targets = dst_local[batch].reshape(N_ACCT, TIL_DEV)
    times = delta_t[batch].reshape(N_ACCT, TIL_DEV)
    tiles = masks[batch].reshape(N_ACCT, TIL_DEV, BLK, BLK)

    def group(items):
        blocks, target, stamp, tile = items
        rows = jnp.take(pre, blocks, axis=1)
        code = jnp.cos(stamp[:, None] * omega[None, :])
        hidden = jax.nn.relu(rows.astype(jnp.float32) + b_msg1 + code[None]).astype(jnp.bfloat16)
        message = jnp.einsum('sth,hd->std', hidden.astype(jnp.float32), w_msg2.astype(jnp.float32)).astype(jnp.bfloat16)
        partial_value = jnp.einsum('tsd,ste->dte', tile.astype(jnp.float32), message.astype(jnp.float32))
        onehot = (target[:, None] == jnp.arange(BLK_DEV, dtype=jnp.int32)[None, :]).astype(jnp.float32)
        return jnp.einsum('dte,tb->dbe', partial_value, onehot)
    agg = lax.map(group, (source, targets, times, tiles))
    agg = jnp.transpose(agg, (1, 0, 2, 3)).reshape(BLK, BLOCKS, D)

    def update(items):
        total, old, flag = items
        mean = lax.optimization_barrier(jnp.mean(total, axis=-1, keepdims=True))
        var = lax.optimization_barrier(jnp.mean((total - mean) ** 2, axis=-1, keepdims=True))
        normed = ((total - mean) * lax.rsqrt(var + 1e-05) * ln_gain).astype(jnp.bfloat16)
        gin = jnp.dot(normed, w_in, preferred_element_type=jnp.float32) + b_in
        ghid = jnp.dot(old, w_hid, preferred_element_type=jnp.float32) + b_hid
        zgate = jax.nn.sigmoid(gin[:, :D] + ghid[:, :D])
        rgate = jax.nn.sigmoid(gin[:, D:2 * D] + ghid[:, D:2 * D])
        cand = jnp.tanh(gin[:, 2 * D:] + rgate * ghid[:, 2 * D:])
        fresh = (1.0 - zgate) * cand + zgate * old.astype(jnp.float32)
        return jnp.where(flag[:, None] == 1, fresh.astype(jnp.bfloat16), old)
    return lax.map(update, (agg, state, member[batch]))

def reference(memory, src_dev, src_local, dst_local, delta_t, masks, member, w_msg1, b_msg1, omega, w_msg2, ln_gain, w_in, w_hid, b_in, b_hid):
    state = memory
    for batch in range(NB):
        state = batch_step(state, batch, src_dev, src_local, dst_local, delta_t, masks, member, w_msg1, b_msg1, omega, w_msg2, ln_gain, w_in, w_hid, b_in, b_hid)
    return state
```

```python
import functools

import jax
import jax.numpy as jnp
from jax import lax
from jax.experimental import pallas as pl
from jax.experimental.pallas import tpu as pltpu
from jax.sharding import PartitionSpec as P

NB = 3
NZ, NX, NC, NR = 8, 4, 2, 4
BD, TD, ROWS, D = 8, 32, 32, 512
CAP = 32
COL = NZ * BD
BF, F32 = jnp.bfloat16, jnp.float32

ANY = pl.BlockSpec(memory_space=pl.ANY)
SMEM = pl.BlockSpec(memory_space=pltpu.SMEM)
VMEM = pl.BlockSpec(memory_space=pltpu.VMEM)


def z_shift(s):
    n = NX * NC
    return [(i, ((i // n + s) % NZ) * n + i % n) for i in range(NZ * n)]


def x_shift(s):
    n = NX * NC
    return [(i, (i // n) * n + ((i // NC + s) % NX) * NC + i % NC) for i in range(NZ * n)]


def core_swap():
    return [(i, i ^ 1) for i in range(NZ * NX * NC)]


def rep_shift(s):
    return [(i, (i + s) % NR) for i in range(NR)]


def start_from(table, place, dst, sem):
    low = 0
    for ref in table:
        high = low + ref.shape[0]

        @pl.when((place >= low) & (place < high))
        def _(ref=ref, low=low):
            pltpu.make_async_copy(ref.at[place - low], dst, sem).start()

        low = high


def pick_kernel(counts, idx_ref, *refs):
    n_out = len(counts)
    sem = refs[-1]
    table = refs[: len(refs) - 1 - n_out]
    outs = refs[len(refs) - 1 - n_out : -1]
    base = 0
    for o, (out, count) in enumerate(zip(outs, counts)):

        def body(s, carry, out=out, base=base, o=o):
            start_from(table, idx_ref[base + s], out.at[s], sem.at[o])
            return carry

        lax.fori_loop(0, count, body, 0)
        base += count
    for o, out in enumerate(outs):
        pltpu.make_async_copy(out, out, sem.at[o]).wait()


def pick(idx, table, counts):
    return pl.pallas_call(
        functools.partial(pick_kernel, counts),
        out_shape=[jax.ShapeDtypeStruct((n, ROWS, D), BF) for n in counts],
        in_specs=[SMEM] + [ANY] * len(table),
        out_specs=[ANY] * len(counts),
        scratch_shapes=[pltpu.SemaphoreType.DMA((len(counts),))],
        name="pick",
    )(idx, *table)


def message_kernel(n_table, rep_ref, idx_ref, code_ref, w2_ref, mask_ref, hot_ref, *refs):
    table = refs[:n_table]
    own_ref, out1, out2, out3, rows_ref, lhs_ref, sem = refs[n_table:]

    def body(t, carry):
        start_from(table, idx_ref[t], rows_ref.at[t], sem)
        return carry

    lax.fori_loop(0, TD, body, 0)
    rep = rep_ref[0]
    for j in range(NR):
        r = lax.rem(rep + j, NR)
        quarter = mask_ref[pl.ds(pl.multiple_of(r * ROWS, ROWS), ROWS), :]
        for k in range(BD):
            lhs_ref[pl.ds((j * BD + k) * ROWS, ROWS), :] = quarter * hot_ref[k : k + 1, :]
    pltpu.make_async_copy(rows_ref, rows_ref, sem).wait()
    hidden = rows_ref[...].astype(F32) + code_ref[...][:, None, :]
    hidden = jnp.maximum(hidden, 0.0).astype(BF).reshape(TD * ROWS, D)
    message = jnp.dot(hidden, w2_ref[...], preferred_element_type=F32).astype(BF)
    agg = jnp.dot(lhs_ref[...], message, preferred_element_type=F32)
    n = BD * ROWS
    own_ref[...] = agg[:n]
    out1[...] = agg[n : 2 * n].astype(BF)
    out2[...] = agg[2 * n : 3 * n].astype(BF)
    out3[...] = agg[3 * n :].astype(BF)


def message_call(rep, idx, code, w2, mask, hot, table):
    n = BD * ROWS
    return pl.pallas_call(
        functools.partial(message_kernel, len(table)),
        out_shape=[jax.ShapeDtypeStruct((n, D), F32)] + [jax.ShapeDtypeStruct((n, D), BF)] * 3,
        in_specs=[SMEM, SMEM, VMEM, VMEM, VMEM, VMEM] + [ANY] * len(table),
        out_specs=[VMEM] * 4,
        scratch_shapes=[
            pltpu.VMEM((TD, ROWS, D), BF),
            pltpu.VMEM((NR * n, TD * ROWS), BF),
            pltpu.SemaphoreType.DMA(()),
        ],
        compiler_params=pltpu.CompilerParams(vmem_limit_bytes=32 << 20),
        name="message",
    )(rep, idx, code, w2, mask, hot, *table)


def sigmoid(v):
    return 0.5 * jnp.tanh(0.5 * v) + 0.5


def update_kernel(last, own, in1, in2, in3, state, member, gain, w_in, w_hid, b_in, b_hid, w1, *outs):
    total = own[...] + in1[...].astype(F32) + in2[...].astype(F32) + in3[...].astype(F32)
    mean = jnp.mean(total, axis=-1, keepdims=True)
    centred = total - mean
    var = jnp.mean(centred * centred, axis=-1, keepdims=True)
    x = (centred * lax.rsqrt(var + 1e-05) * gain[...]).astype(BF)
    old = state[...]
    gin = jnp.dot(x, w_in[...], preferred_element_type=F32) + b_in[...]
    ghid = jnp.dot(old, w_hid[...], preferred_element_type=F32) + b_hid[...]
    z = sigmoid(gin[:, :D] + ghid[:, :D])
    r = sigmoid(gin[:, D : 2 * D] + ghid[:, D : 2 * D])
    cand = jnp.tanh(gin[:, 2 * D :] + r * ghid[:, 2 * D :])
    fresh = (1.0 - z) * cand + z * old.astype(F32)
    new = jnp.where(member[...] == 1, fresh, old.astype(F32)).astype(BF)
    outs[0][...] = new
    if not last:
        outs[1][...] = jnp.dot(new, w1[...], preferred_element_type=F32).astype(BF)


def update_call(last, *args):
    n = BD * ROWS
    outs = [jax.ShapeDtypeStruct((n, D), BF)] * (1 if last else 2)
    return pl.pallas_call(
        functools.partial(update_kernel, last),
        out_shape=outs,
        in_specs=[VMEM] * len(args),
        out_specs=[VMEM] * len(outs),
        compiler_params=pltpu.CompilerParams(vmem_limit_bytes=32 << 20),
        name="update",
    )(*args)


def first_kernel(state, w1, pre):
    pre[...] = jnp.dot(state[...], w1[...], preferred_element_type=F32).astype(BF)


def first_call(state, w1):
    return pl.pallas_call(
        first_kernel,
        out_shape=jax.ShapeDtypeStruct(state.shape, BF),
        in_specs=[VMEM] * 2,
        out_specs=VMEM,
        name="first",
    )(state, w1)


def places(src_dev, src_local):
    me = lax.axis_index("acct")
    z, x, c = me // (NX * NC), (me // NC) % NX, me % NC
    dev = src_dev.reshape(NB, NZ, NX, NC * TD)
    loc = src_local.reshape(NB, NZ, NX, NC * TD)
    dev = lax.dynamic_slice_in_dim(dev, z, 1, 1)[:, 0]
    loc = lax.dynamic_slice_in_dim(loc, z, 1, 1)[:, 0]
    sz, sx, sc = dev // (NX * NC), (dev // NC) % NX, dev % NC
    column = ((sz - z) % NZ) * BD + loc
    pair = sx * NC + sc
    tile = jnp.arange(NC * TD, dtype=jnp.int32)
    before = (tile[None, :] < tile[:, None]).astype(jnp.int32)
    rank = jnp.sum((pair[..., :, None] == pair[..., None, :]) * before, axis=-1)
    mine = pair == x * NC + c
    slots = jnp.arange(CAP, dtype=jnp.int32)
    chosen = mine[:, :, None, :] & (rank[:, :, None, :] == slots[None, None, :, None])
    out = jnp.sum(jnp.where(chosen, column[:, :, None, :], 0), axis=-1)
    lanes = (x + jnp.arange(1, NX, dtype=jnp.int32)) % NX
    turn = (lanes[:, None] == jnp.arange(NX, dtype=jnp.int32)[None, :]).astype(jnp.int32)
    send = jnp.sum(out[:, None, :, :] * turn[None, :, :, None], axis=2).reshape(NB, -1)
    here = (jnp.arange(NX, dtype=jnp.int32) == x).astype(jnp.int32)[None, :, None]
    column, rank, sx, sc = (jnp.sum(a * here, axis=1) for a in (column, rank, sx, sc))
    lane = (sx - x) % NX
    place = jnp.where(lane == 0, column, COL + (lane - 1) * CAP + rank)
    place = place.reshape(NB, NC, TD)
    local = (sc == c).reshape(NB, NC, TD)
    self_ = (jnp.arange(NC, dtype=jnp.int32) == c).astype(jnp.int32)[None, :, None]
    swapped = COL + (NX - 1) * CAP + jnp.arange(TD, dtype=jnp.int32)
    final = jnp.sum(jnp.where(local, place, swapped[None, None]) * self_, axis=1)
    swap = jnp.sum(jnp.where(local, place, 0) * (1 - self_), axis=1)
    return send, swap, final


def exchange(pre, send, swap):
    up, down = [pre], [pre]
    for step in range(3):
        up.append(lax.ppermute(up[-1], "acct", z_shift(1)))
        down.append(lax.ppermute(down[-1], "acct", z_shift(-1)))
    half = BD // 2
    far_up = lax.ppermute(up[3][:half], "acct", z_shift(1))
    far_down = lax.ppermute(down[3][half:], "acct", z_shift(-1))
    column = [pre, down[1], down[2], down[3], far_up, far_down, up[3], up[2], up[1]]
    outgoing = pick(send, column, (CAP,) * (NX - 1))
    arrived = [lax.ppermute(outgoing[d - 1], "acct", x_shift(d)) for d in range(1, NX)]
    table = column + arrived[::-1]
    [crossing] = pick(swap, table, (TD,))
    return table + [lax.ppermute(crossing, "acct", core_swap())]


def per_device(
    memory, src_dev, src_local, dst_local, delta_t, masks, member,
    w_msg1, b_msg1, omega, w_msg2, ln_gain, w_in, w_hid, b_in, b_hid,
):
    n = BD * ROWS
    rep = lax.axis_index("rep").reshape(1).astype(jnp.int32)
    state = jnp.swapaxes(memory, 0, 1).reshape(n, D)
    pre = first_call(state, w_msg1)
    send, swap, final = places(src_dev, src_local)
    code = jnp.cos(delta_t[:, :, None] * omega) + b_msg1
    mask = jnp.transpose(masks, (0, 3, 1, 2)).reshape(NB, NR * ROWS, TD * ROWS).astype(BF)
    hot = dst_local[:, None, :] == jnp.arange(BD, dtype=jnp.int32)[None, :, None]
    hot = jnp.repeat(hot.astype(BF), ROWS, axis=2)
    chosen = jnp.swapaxes(member, 1, 2).reshape(NB, n, 1)
    for batch in range(NB):
        table = exchange(pre.reshape(BD, ROWS, D), send[batch], swap[batch])
        own, *shares = message_call(
            rep, final[batch], code[batch], w_msg2, mask[batch], hot[batch], table
        )
        shares = [lax.ppermute(s, "rep", rep_shift(j + 1)) for j, s in enumerate(shares)]
        last = batch == NB - 1
        state, *rest = update_call(
            last, own, *shares, state, chosen[batch], ln_gain[None], w_in, w_hid, b_in[None], b_hid[None], w_msg1
        )
        if not last:
            pre = rest[0]
    return jnp.swapaxes(state.reshape(BD, ROWS, D), 0, 1)


def solution(mesh):
    placed = (
        P("rep", "acct", None),
        P(),
        P(),
        P(None, "acct"),
        P(None, "acct"),
        P(None, "acct", "rep", None),
        P(None, "rep", "acct"),
    ) + (P(),) * 9
    return jax.shard_map(
        per_device, mesh=mesh, in_specs=placed, out_specs=P("rep", "acct", None), check_vma=False
    )
```

```python
import functools

import jax
import jax.numpy as jnp
from jax import lax
from jax.experimental import pallas as pl
from jax.experimental.pallas import tpu as pltpu
from jax.sharding import PartitionSpec as P

NB = 3
NZ, NX, NC, NR = 8, 4, 2, 4
BD, TD, ROWS, D = 8, 32, 32, 512
SLOTS = 16
CAP = 2 * SLOTS
COL = NZ * BD
BF, F32 = jnp.bfloat16, jnp.float32

SMEM = pl.BlockSpec(memory_space=pltpu.SMEM)
VMEM = pl.BlockSpec(memory_space=pltpu.VMEM)


def z_shift(s):
    n = NX * NC
    return [(i, ((i // n + s) % NZ) * n + i % n) for i in range(NZ * n)]


def x_shift(s):
    n = NX * NC
    return [(i, (i // n) * n + ((i // NC + s) % NX) * NC + i % NC) for i in range(NZ * n)]


def core_swap():
    return [(i, i ^ 1) for i in range(NZ * NX * NC)]


def rep_shift(s):
    return [(i, (i + s) % NR) for i in range(NR)]


def copy_from(table, place, put):
    low = 0
    for ref in table:
        high = low + ref.shape[0]

        @pl.when((place >= low) & (place < high))
        def _(ref=ref, low=low):
            put(ref[place - low])

        low = high


def gather_kernel(batch, base, n_column, idx_ref, *refs):
    pieces, outs = refs[:n_column], refs[n_column:]
    if n_column > 1:
        column, lanes = outs[0], outs[1:]
        low = 0
        for piece in pieces:
            column[low : low + piece.shape[0]] = piece[...]
            low += piece.shape[0]
    else:
        column, lanes = pieces[0], outs
    for d, lane in enumerate(lanes):

        def body(s, carry, lane=lane, d=d):
            lane[s] = column[idx_ref[batch, d * CAP + base + s]]
            return carry

        lax.fori_loop(0, lane.shape[0], body, 0, unroll=4)


def gather_call(batch, base, idx, pieces):
    lanes = [jax.ShapeDtypeStruct((SLOTS, ROWS, D), BF)] * (NX - 1)
    column = [jax.ShapeDtypeStruct((COL, ROWS, D), BF)] if len(pieces) > 1 else []
    return pl.pallas_call(
        functools.partial(gather_kernel, batch, base, len(pieces)),
        out_shape=column + lanes,
        in_specs=[SMEM] + [VMEM] * len(pieces),
        out_specs=[VMEM] * len(column + lanes),
        compiler_params=pltpu.CompilerParams(vmem_limit_bytes=32 << 20),
        name="gather",
    )(idx, *pieces)


def swap_kernel(batch, idx_ref, *refs):
    table, out = refs[:-1], refs[-1]

    def body(t, carry):
        def put(block):
            out[t] = block

        copy_from(table, idx_ref[batch, t], put)
        return carry

    lax.fori_loop(0, TD, body, 0)


def swap_call(batch, idx, table):
    return pl.pallas_call(
        functools.partial(swap_kernel, batch),
        out_shape=jax.ShapeDtypeStruct((TD, ROWS, D), BF),
        in_specs=[SMEM] + [VMEM] * len(table),
        out_specs=VMEM,
        compiler_params=pltpu.CompilerParams(vmem_limit_bytes=32 << 20),
        name="swap",
    )(idx, *table)


def prepare_kernel(masks_ref, dst_ref, mask_ref, hot_ref):
    tile = lax.broadcasted_iota(jnp.int32, (TD, TD * ROWS), 0)
    place = lax.broadcasted_iota(jnp.int32, (TD, TD * ROWS), 1)
    spread = ((place >= tile * ROWS) & (place < (tile + 1) * ROWS)).astype(BF)
    for batch in range(NB):
        bits = masks_ref[batch].astype(F32).reshape(TD * ROWS, NR * ROWS)
        mask_ref[batch] = bits.T.astype(BF)
        block = lax.broadcasted_iota(jnp.int32, (BD, TD), 0)
        hot = (dst_ref[batch : batch + 1, :] == block).astype(BF)
        hot_ref[batch] = jnp.dot(hot, spread, preferred_element_type=F32).astype(BF)


def prepare_call(masks, dst):
    return pl.pallas_call(
        prepare_kernel,
        out_shape=[
            jax.ShapeDtypeStruct((NB, NR * ROWS, TD * ROWS), BF),
            jax.ShapeDtypeStruct((NB, BD, TD * ROWS), BF),
        ],
        in_specs=[VMEM] * 2,
        out_specs=[VMEM] * 2,
        compiler_params=pltpu.CompilerParams(vmem_limit_bytes=32 << 20),
        name="prepare",
    )(masks, dst)


def message_kernel(batch, n_table, rep_ref, idx_ref, code_ref, w2_ref, mask_ref, hot_ref, *refs):
    table = refs[:n_table]
    own_ref, out1, out2, out3, hidden_ref, lhs_ref = refs[n_table:]

    def body(t, carry):
        def put(block):
            code = code_ref[batch, pl.ds(t, 1), :]
            hidden_ref[t] = jnp.maximum(block.astype(F32) + code, 0.0).astype(BF)

        copy_from(table, idx_ref[batch, t], put)
        return carry

    lax.fori_loop(0, TD, body, 0)
    rep = rep_ref[0]
    for j in range(NR):
        r = lax.rem(rep + j, NR)
        quarter = mask_ref[batch, pl.ds(pl.multiple_of(r * ROWS, ROWS), ROWS), :]
        for k in range(BD):
            lhs_ref[pl.ds((j * BD + k) * ROWS, ROWS), :] = quarter * hot_ref[batch, k : k + 1, :]
    hidden = hidden_ref[...].reshape(TD * ROWS, D)
    message = jnp.dot(hidden, w2_ref[...], preferred_element_type=F32).astype(BF)
    agg = jnp.dot(lhs_ref[...], message, preferred_element_type=F32)
    n = BD * ROWS
    own_ref[...] = agg[:n]
    out1[...] = agg[n : 2 * n].astype(BF)
    out2[...] = agg[2 * n : 3 * n].astype(BF)
    out3[...] = agg[3 * n :].astype(BF)


def message_call(batch, rep, idx, code, w2, mask, hot, table):
    n = BD * ROWS
    return pl.pallas_call(
        functools.partial(message_kernel, batch, len(table)),
        out_shape=[jax.ShapeDtypeStruct((n, D), F32)] + [jax.ShapeDtypeStruct((n, D), BF)] * 3,
        in_specs=[SMEM, SMEM] + [VMEM] * (4 + len(table)),
        out_specs=[VMEM] * 4,
        scratch_shapes=[
            pltpu.VMEM((TD, ROWS, D), BF),
            pltpu.VMEM((NR * n, TD * ROWS), BF),
        ],
        compiler_params=pltpu.CompilerParams(vmem_limit_bytes=32 << 20),
        name="message",
    )(rep, idx, code, w2, mask, hot, *table)


def sigmoid(v):
    return 0.5 * jnp.tanh(0.5 * v) + 0.5


def update_kernel(batch, last, own, in1, in2, in3, state, member, gain, w_in, w_hid, b_in, b_hid, w1, *outs):
    total = own[...] + in1[...].astype(F32) + in2[...].astype(F32) + in3[...].astype(F32)
    mean = jnp.mean(total, axis=-1, keepdims=True)
    centred = total - mean
    var = jnp.mean(centred * centred, axis=-1, keepdims=True)
    x = (centred * lax.rsqrt(var + 1e-05) * gain[...]).astype(BF)
    old = state[...]
    gin = jnp.dot(x, w_in[...], preferred_element_type=F32) + b_in[...]
    ghid = jnp.dot(old, w_hid[...], preferred_element_type=F32) + b_hid[...]
    z = sigmoid(gin[:, :D] + ghid[:, :D])
    r = sigmoid(gin[:, D : 2 * D] + ghid[:, D : 2 * D])
    cand = jnp.tanh(gin[:, 2 * D :] + r * ghid[:, 2 * D :])
    fresh = (1.0 - z) * cand + z * old.astype(F32)
    new = jnp.where(member[batch] == 1, fresh, old.astype(F32)).astype(BF)
    outs[0][...] = new
    if not last:
        outs[1][...] = jnp.dot(new, w1[...], preferred_element_type=F32).astype(BF)


def update_call(batch, last, *args):
    n = BD * ROWS
    outs = [jax.ShapeDtypeStruct((n, D), BF)] * (1 if last else 2)
    return pl.pallas_call(
        functools.partial(update_kernel, batch, last),
        out_shape=outs,
        in_specs=[VMEM] * len(args),
        out_specs=[VMEM] * len(outs),
        compiler_params=pltpu.CompilerParams(vmem_limit_bytes=32 << 20),
        name="update",
    )(*args)


def first_kernel(state, w1, pre):
    pre[...] = jnp.dot(state[...], w1[...], preferred_element_type=F32).astype(BF)


def first_call(state, w1):
    return pl.pallas_call(
        first_kernel,
        out_shape=jax.ShapeDtypeStruct(state.shape, BF),
        in_specs=[VMEM] * 2,
        out_specs=VMEM,
        name="first",
    )(state, w1)


def ranks(dev, loc):
    tile = jnp.arange(NC * TD, dtype=jnp.int32)
    before = tile[None, :] < tile[:, None]
    pair = dev % (NX * NC)
    lane = pair[..., :, None] == pair[..., None, :]
    block = dev * BD + loc
    same = block[..., :, None] == block[..., None, :]
    first = ~jnp.any(same & before, axis=-1)
    new = jnp.where(before & lane & first[..., None, :], 1, 0)
    rank = jnp.sum(new, axis=-1)
    home = jnp.sum(jnp.where(same & first[..., None, :], rank[..., None, :], 0), axis=-1)
    return home


def places(src_dev, src_local):
    me = lax.axis_index("acct")
    z, x, c = me // (NX * NC), (me // NC) % NX, me % NC
    dev = src_dev.reshape(NB, NZ, NX, NC * TD)
    loc = src_local.reshape(NB, NZ, NX, NC * TD)
    away = (dev // NC) % NX != jnp.arange(NX, dtype=jnp.int32)[None, None, :, None]
    deepest = jnp.max(jnp.where(away, ranks(dev, loc), 0), axis=(1, 2, 3))
    dev = lax.dynamic_slice_in_dim(dev, z, 1, 1)[:, 0]
    loc = lax.dynamic_slice_in_dim(loc, z, 1, 1)[:, 0]
    sz, sx, sc = dev // (NX * NC), (dev // NC) % NX, dev % NC
    column = ((sz - z) % NZ) * BD + loc
    rank = ranks(dev, loc)
    mine = sx * NC + sc == x * NC + c
    slots = jnp.arange(CAP, dtype=jnp.int32)
    chosen = mine[:, :, None, :] & (rank[:, :, None, :] == slots[None, None, :, None])
    out = jnp.max(jnp.where(chosen, column[:, :, None, :], 0), axis=-1)
    lanes = (x + jnp.arange(1, NX, dtype=jnp.int32)) % NX
    turn = (lanes[:, None] == jnp.arange(NX, dtype=jnp.int32)[None, :]).astype(jnp.int32)
    send = jnp.sum(out[:, None, :, :] * turn[None, :, :, None], axis=2).reshape(NB, -1)
    here = (jnp.arange(NX, dtype=jnp.int32) == x).astype(jnp.int32)[None, :, None]
    column, rank, sx, sc = (jnp.sum(a * here, axis=1) for a in (column, rank, sx, sc))
    lane = (sx - x) % NX
    early = COL + (lane - 1) * SLOTS + rank
    place = jnp.where(rank < SLOTS, early, early + (NX - 2) * SLOTS)
    place = jnp.where(lane == 0, column, place).reshape(NB, NC, TD)
    local = (sc == c).reshape(NB, NC, TD)
    self_ = (jnp.arange(NC, dtype=jnp.int32) == c).astype(jnp.int32)[None, :, None]
    swapped = COL + (NX - 1) * CAP + jnp.arange(TD, dtype=jnp.int32)
    final = jnp.sum(jnp.where(local, place, swapped[None, None]) * self_, axis=1)
    swap = jnp.sum(jnp.where(local, place, 0) * (1 - self_), axis=1)
    return send, swap, final, deepest >= SLOTS


def along_x(lanes):
    return [lax.ppermute(lanes[d - 1], "acct", x_shift(d)) for d in range(NX - 1, 0, -1)]


def exchange(batch, pre, send, swap, more):
    up, down = [pre], [pre]
    for step in range(3):
        up.append(lax.ppermute(up[-1], "acct", z_shift(1)))
        down.append(lax.ppermute(down[-1], "acct", z_shift(-1)))
    half = BD // 2
    far_up = lax.ppermute(up[3][:half], "acct", z_shift(1))
    far_down = lax.ppermute(down[3][half:], "acct", z_shift(-1))
    column, *lanes = gather_call(
        batch, 0, send, [pre, down[1], down[2], down[3], far_up, far_down, up[3], up[2], up[1]]
    )
    early = along_x(lanes)
    late = lax.cond(
        more[batch],
        lambda: along_x(gather_call(batch, SLOTS, send, [column])),
        lambda: [jnp.zeros((SLOTS, ROWS, D), BF)] * (NX - 1),
    )
    table = [column, *early, *late]
    return table + [lax.ppermute(swap_call(batch, swap, table), "acct", core_swap())]


def per_device(
    memory, src_dev, src_local, dst_local, delta_t, masks, member,
    w_msg1, b_msg1, omega, w_msg2, ln_gain, w_in, w_hid, b_in, b_hid,
):
    n = BD * ROWS
    rep = lax.axis_index("rep").reshape(1).astype(jnp.int32)
    state = jnp.swapaxes(memory, 0, 1).reshape(n, D)
    pre = first_call(state, w_msg1)
    send, swap, final, more = places(src_dev, src_local)
    code = jnp.cos(delta_t[:, :, None] * omega) + b_msg1
    mask, hot = prepare_call(masks, dst_local)
    chosen = jnp.swapaxes(member, 1, 2).reshape(NB, n, 1)
    for batch in range(NB):
        table = exchange(batch, pre.reshape(BD, ROWS, D), send, swap, more)
        own, *shares = message_call(batch, rep, final, code, w_msg2, mask, hot, table)
        shares = [lax.ppermute(s, "rep", rep_shift(j + 1)) for j, s in enumerate(shares)]
        last = batch == NB - 1
        state, *rest = update_call(
            batch, last, own, *shares, state, chosen, ln_gain[None], w_in, w_hid, b_in[None], b_hid[None], w_msg1
        )
        if not last:
            pre = rest[0]
    return jnp.swapaxes(state.reshape(BD, ROWS, D), 0, 1)


def solution(mesh):
    placed = (
        P("rep", "acct", None),
        P(),
        P(),
        P(None, "acct"),
        P(None, "acct"),
        P(None, "acct", "rep", None),
        P(None, "rep", "acct"),
    ) + (P(),) * 9
    return jax.shard_map(
        per_device, mesh=mesh, in_specs=placed, out_specs=P("rep", "acct", None), check_vma=False
    )
```

```python
import functools

import jax
import jax.numpy as jnp
from jax import lax
from jax.experimental import pallas as pl
from jax.experimental.pallas import tpu as pltpu
from jax.sharding import PartitionSpec as P

NB = 3
NZ, NX, NC, NR = 8, 4, 2, 4
BD, TD, ROWS, D = 8, 32, 32, 512
PARTS = 2
PR = ROWS // PARTS
SLOTS = 16
CAP = 2 * SLOTS
COL = NZ * BD
EARLY = COL + (NX - 1) * SLOTS
BF, F32, I32 = jnp.bfloat16, jnp.float32, jnp.int32

SMEM = pl.BlockSpec(memory_space=pltpu.SMEM)
VMEM = pl.BlockSpec(memory_space=pltpu.VMEM)


def call(kernel, name, outs, specs, args, scratch=()):
    many = isinstance(outs, list)
    return pl.pallas_call(
        kernel,
        out_shape=outs,
        in_specs=specs,
        out_specs=[VMEM] * len(outs) if many else VMEM,
        scratch_shapes=scratch,
        compiler_params=pltpu.CompilerParams(vmem_limit_bytes=20 << 20),
        name=name,
    )(*args)


def shape(*dims, dtype=BF):
    return jax.ShapeDtypeStruct(dims, dtype)


def z_shift(s):
    n = NX * NC
    return [(i, ((i // n + s) % NZ) * n + i % n) for i in range(NZ * n)]


def x_shift(s):
    n = NX * NC
    return [(i, (i // n) * n + ((i // NC + s) % NX) * NC + i % NC) for i in range(NZ * n)]


def core_swap():
    return [(i, i ^ 1) for i in range(NZ * NX * NC)]


def rep_shift(s):
    return [(i, (i + s) % NR) for i in range(NR)]


def early_block(place, column, lanes):
    block = column[jnp.clip(place, 0, COL - 1)]
    for d, lane in enumerate(lanes):
        low = COL + d * SLOTS
        slot = jnp.clip(place - low, 0, SLOTS - 1)
        block = jnp.where((place >= low) & (place < low + SLOTS), lane[slot], block)
    return block


def late_block(place, late, put):
    for d, lane in enumerate(late):
        low = EARLY + d * SLOTS

        @pl.when((place >= low) & (place < low + SLOTS))
        def _(lane=lane, low=low):
            put(lane[place - low])


def gather_kernel(batch, base, n_column, idx_ref, *refs):
    pieces, outs = refs[:n_column], refs[n_column:]
    if n_column > 1:
        column, lanes = outs[0], outs[1:]
        low = 0
        for piece in pieces:
            column[low : low + piece.shape[0]] = piece[...]
            low += piece.shape[0]
    else:
        column, lanes = pieces[0], outs
    for s in range(SLOTS):
        for d, lane in enumerate(lanes):
            lane[s] = column[idx_ref[batch, d * CAP + base + s]]


def gather_call(batch, base, idx, pieces):
    outs = [shape(COL, PR, D)] if len(pieces) > 1 else []
    return call(
        functools.partial(gather_kernel, batch, base, len(pieces)),
        "gather",
        outs + [shape(SLOTS, PR, D)] * (NX - 1),
        [SMEM] + [VMEM] * len(pieces),
        (idx, *pieces),
    )


def swap_kernel(batch, idx_ref, more_ref, column, *refs):
    lanes, late, out = refs[: NX - 1], refs[NX - 1 : -1], refs[-1]
    for t in range(TD):
        out[t] = early_block(idx_ref[batch, t], column, lanes)

    @pl.when(more_ref[batch] == 1)
    def _():
        def body(t, carry):
            def put(block):
                out[t] = block

            late_block(idx_ref[batch, t], late, put)
            return carry

        lax.fori_loop(0, TD, body, 0)


def swap_call(batch, idx, more, table):
    return call(
        functools.partial(swap_kernel, batch),
        "swap",
        shape(TD, PR, D),
        [SMEM] * 2 + [VMEM] * len(table),
        (idx, more, *table),
    )


def hidden_of(block, code):
    return jnp.maximum(block.astype(F32) + code, 0.0).astype(BF)


def local_kernel(batch, idx_ref, more_ref, code_ref, column, *refs):
    lanes, late, out = refs[: NX - 1], refs[NX - 1 : -1], refs[-1]
    for t in range(TD):
        block = early_block(idx_ref[batch, t], column, lanes)
        out[t] = hidden_of(block, code_ref[batch, t : t + 1, :])

    @pl.when(more_ref[batch] == 1)
    def _():
        def body(t, carry):
            def put(block):
                out[t] = hidden_of(block, code_ref[batch, pl.ds(t, 1), :])

            late_block(idx_ref[batch, t], late, put)
            return carry

        lax.fori_loop(0, TD, body, 0)


def local_call(batch, idx, more, code, table):
    return call(
        functools.partial(local_kernel, batch),
        "local",
        shape(TD, PR, D),
        [SMEM] * 2 + [VMEM] * (1 + len(table)),
        (idx, more, code, *table),
    )


def message_kernel(batch, idx_ref, code_ref, w2_ref, local_ref, swapped_ref, out_ref, hidden_ref):
    for t in range(TD):
        crossed = hidden_of(swapped_ref[t], code_ref[batch, t : t + 1, :])
        hidden_ref[t] = jnp.where(idx_ref[batch, t] >= 0, local_ref[t], crossed)
    hidden = hidden_ref[...].reshape(TD * PR, D)
    out_ref[...] = jnp.dot(hidden, w2_ref[...], preferred_element_type=F32).astype(BF)


def message_call(batch, idx, code, w2, local, swapped):
    return call(
        functools.partial(message_kernel, batch),
        "message",
        shape(TD * PR, D),
        [SMEM] + [VMEM] * 4,
        (idx, code, w2, local, swapped),
        [pltpu.VMEM((TD, PR, D), BF)],
    )


def sum_kernel(lhs_ref, *refs):
    messages, outs = refs[:PARTS], refs[PARTS:]
    n, depth = BD * PR, TD * PR
    agg = 0.0
    for p, message in enumerate(messages):
        lhs = lhs_ref[:, p * depth : (p + 1) * depth]
        agg = agg + jnp.dot(lhs, message[...], preferred_element_type=F32)
    outs[0][...] = agg[:n]
    for j in range(1, NR):
        outs[j][...] = agg[j * n : (j + 1) * n].astype(BF)


def sum_call(lhs, messages):
    n = BD * PR
    return call(
        sum_kernel,
        "sum",
        [shape(n, D, dtype=F32)] + [shape(n, D)] * (NR - 1),
        [VMEM] * (1 + PARTS),
        (lhs, *messages),
    )


def prepare_kernel(rep_ref, masks_ref, dst_ref, *outs):
    mask_ref = outs[-1]
    outs = outs[:-1]
    depth = TD * PR
    tile = lax.broadcasted_iota(I32, (TD, depth), 0)
    place = lax.broadcasted_iota(I32, (TD, depth), 1)
    spread = ((place >= tile * PR) & (place < (tile + 1) * PR)).astype(BF)
    block = lax.broadcasted_iota(I32, (BD, TD), 0)
    rep = rep_ref[0]
    for batch in range(NB):
        hot = (dst_ref[batch : batch + 1, :] == block).astype(BF)
        hot = jnp.dot(hot, spread, preferred_element_type=F32).astype(BF)
        for p in range(PARTS):
            bits = masks_ref[batch, :, p * PR : (p + 1) * PR, :].astype(F32)
            mask_ref[:, p * depth : (p + 1) * depth] = bits.reshape(depth, NR * ROWS).T.astype(BF)
        for j in range(NR):
            r = lax.rem(rep + j, NR)
            for q in range(PARTS):
                rows = mask_ref[pl.ds(pl.multiple_of(r * ROWS + q * PR, PR), PR), :]
                for k in range(BD):
                    low = (j * BD + k) * PR
                    for p in range(PARTS):
                        part = rows[:, p * depth : (p + 1) * depth]
                        outs[batch * PARTS + q][low : low + PR, p * depth : (p + 1) * depth] = part * hot[k : k + 1, :]


def prepare_call(rep, masks, dst):
    return call(
        prepare_kernel,
        "prepare",
        [shape(NR * BD * PR, TD * ROWS)] * (NB * PARTS),
        [SMEM] + [VMEM] * 2,
        (rep, masks, dst),
        [pltpu.VMEM((NR * ROWS, TD * ROWS), BF)],
    )


def sigmoid(v):
    return 0.5 * jnp.tanh(0.5 * v) + 0.5


def update_kernel(batch, part, last, own, in1, in2, in3, state, member, gain, w_in, w_hid, b_in, b_hid, w1, *outs):
    total = own[...] + in1[...].astype(F32) + in2[...].astype(F32) + in3[...].astype(F32)
    mean = jnp.mean(total, axis=-1, keepdims=True)
    centred = total - mean
    var = jnp.mean(centred * centred, axis=-1, keepdims=True)
    x = (centred * lax.rsqrt(var + 1e-05) * gain[...]).astype(BF)
    old = state[...]
    gin = jnp.dot(x, w_in[...], preferred_element_type=F32) + b_in[...]
    ghid = jnp.dot(old, w_hid[...], preferred_element_type=F32) + b_hid[...]
    z = sigmoid(gin[:, :D] + ghid[:, :D])
    r = sigmoid(gin[:, D : 2 * D] + ghid[:, D : 2 * D])
    cand = jnp.tanh(gin[:, 2 * D :] + r * ghid[:, 2 * D :])
    fresh = (1.0 - z) * cand + z * old.astype(F32)
    new = jnp.where(member[batch, part] == 1, fresh, old.astype(F32)).astype(BF)
    outs[0][...] = new
    if not last:
        outs[1][...] = jnp.dot(new, w1[...], preferred_element_type=F32).astype(BF)


def update_call(batch, part, last, *args):
    return call(
        functools.partial(update_kernel, batch, part, last),
        "update",
        [shape(BD * PR, D)] * (1 if last else 2),
        [VMEM] * len(args),
        args,
    )


def first_kernel(state_ref, w1, *outs):
    for p in range(PARTS):
        state = state_ref[:, p * PR : (p + 1) * PR, :].reshape(BD * PR, D)
        outs[p][...] = jnp.dot(state, w1[...], preferred_element_type=F32).astype(BF)
        outs[PARTS + p][...] = state


def first_call(state, w1):
    return call(first_kernel, "first", [shape(BD * PR, D)] * (2 * PARTS), [VMEM] * 2, (state, w1))


def ranks(dev, loc):
    tile = jnp.arange(NC * TD, dtype=I32)
    before = tile[None, :] < tile[:, None]
    pair = dev % (NX * NC)
    lane = pair[..., :, None] == pair[..., None, :]
    block = dev * BD + loc
    same = block[..., :, None] == block[..., None, :]
    first = ~jnp.any(same & before, axis=-1)
    new = jnp.where(before & lane & first[..., None, :], 1, 0)
    rank = jnp.sum(new, axis=-1)
    home = jnp.sum(jnp.where(same & first[..., None, :], rank[..., None, :], 0), axis=-1)
    return home


def places(src_dev, src_local):
    me = lax.axis_index("acct")
    z, x, c = me // (NX * NC), (me // NC) % NX, me % NC
    dev = src_dev.reshape(NB, NZ, NX, NC * TD)
    loc = src_local.reshape(NB, NZ, NX, NC * TD)
    away = (dev // NC) % NX != jnp.arange(NX, dtype=I32)[None, None, :, None]
    deepest = jnp.max(jnp.where(away, ranks(dev, loc), 0), axis=(1, 2, 3))
    dev = lax.dynamic_slice_in_dim(dev, z, 1, 1)[:, 0]
    loc = lax.dynamic_slice_in_dim(loc, z, 1, 1)[:, 0]
    sz, sx, sc = dev // (NX * NC), (dev // NC) % NX, dev % NC
    column = ((sz - z) % NZ) * BD + loc
    rank = ranks(dev, loc)
    mine = sx * NC + sc == x * NC + c
    slots = jnp.arange(CAP, dtype=I32)
    chosen = mine[:, :, None, :] & (rank[:, :, None, :] == slots[None, None, :, None])
    out = jnp.max(jnp.where(chosen, column[:, :, None, :], 0), axis=-1)
    lanes = (x + jnp.arange(1, NX, dtype=I32)) % NX
    turn = (lanes[:, None] == jnp.arange(NX, dtype=I32)[None, :]).astype(I32)
    send = jnp.sum(out[:, None, :, :] * turn[None, :, :, None], axis=2).reshape(NB, -1)
    here = (jnp.arange(NX, dtype=I32) == x).astype(I32)[None, :, None]
    column, rank, sx, sc = (jnp.sum(a * here, axis=1) for a in (column, rank, sx, sc))
    lane = (sx - x) % NX
    early = COL + (lane - 1) * SLOTS + rank
    place = jnp.where(rank < SLOTS, early, early + (NX - 2) * SLOTS)
    place = jnp.where(lane == 0, column, place).reshape(NB, NC, TD)
    local = (sc == c).reshape(NB, NC, TD)
    self_ = (jnp.arange(NC, dtype=I32) == c).astype(I32)[None, :, None]
    final = jnp.sum(jnp.where(local, place, -1) * self_, axis=1)
    swap = jnp.sum(jnp.where(local, place, 0) * (1 - self_), axis=1)
    return send, swap, final, (deepest >= SLOTS).astype(I32)


def along_x(lanes):
    order = [2, 1, 3]
    got = {d: lax.ppermute(lanes[d - 1], "acct", x_shift(d)) for d in order}
    return [got[d] for d in range(NX - 1, 0, -1)]


def along_z(pre):
    up, down = [pre], [pre]
    for step in range(3):
        up.append(lax.ppermute(up[-1], "acct", z_shift(1)))
        down.append(lax.ppermute(down[-1], "acct", z_shift(-1)))
    half = BD // 2
    far_up = lax.ppermute(up[3][:half], "acct", z_shift(1))
    far_down = lax.ppermute(down[3][half:], "acct", z_shift(-1))
    return [pre, down[1], down[2], down[3], far_up, far_down, up[3], up[2], up[1]]


def messages_of(batch, pre, send, swap, final, more, code, w2):
    column, *lanes = gather_call(batch, 0, send, along_z(pre.reshape(BD, PR, D)))
    early = along_x(lanes)
    late = lax.cond(
        more[batch] == 1,
        lambda: along_x(gather_call(batch, SLOTS, send, [column])),
        lambda: [jnp.zeros((SLOTS, PR, D), BF)] * (NX - 1),
    )
    table = [column, *early, *late]
    swapped = lax.ppermute(swap_call(batch, swap, more, table), "acct", core_swap())
    local = local_call(batch, final, more, code, table)
    return message_call(batch, final, code, w2, local, swapped)


def per_device(
    memory, src_dev, src_local, dst_local, delta_t, masks, member,
    w_msg1, b_msg1, omega, w_msg2, ln_gain, w_in, w_hid, b_in, b_hid,
):
    rep = lax.axis_index("rep").reshape(1).astype(I32)
    first = first_call(jnp.swapaxes(memory, 0, 1), w_msg1)
    pre, state = first[:PARTS], first[PARTS:]
    send, swap, final, more = places(src_dev, src_local)
    code = jnp.cos(delta_t[:, :, None] * omega) + b_msg1
    lhs = prepare_call(rep, masks, dst_local)
    chosen = jnp.transpose(member.reshape(NB, PARTS, PR, BD), (0, 1, 3, 2)).reshape(NB, PARTS, BD * PR, 1)
    for batch in range(NB):
        last = batch == NB - 1
        messages = [messages_of(batch, p, send, swap, final, more, code, w_msg2) for p in pre]
        sums = [sum_call(lhs[batch * PARTS + q], messages) for q in range(PARTS)]
        results = []
        for q in range(PARTS):
            own, *shares = sums[q]
            got = {j: lax.ppermute(shares[j - 1], "rep", rep_shift(j)) for j in (2, 1, 3)}
            results.append(
                update_call(
                    batch, q, last, own, got[1], got[2], got[3], state[q], chosen, ln_gain[None],
                    w_in, w_hid, b_in[None], b_hid[None], w_msg1,
                )
            )
        state = [r[0] for r in results]
        pre = [r[-1] for r in results]
    whole = jnp.concatenate([s.reshape(BD, PR, D) for s in state], axis=1)
    return jnp.swapaxes(whole, 0, 1)


def solution(mesh):
    placed = (
        P("rep", "acct", None),
        P(),
        P(),
        P(None, "acct"),
        P(None, "acct"),
        P(None, "acct", "rep", None),
        P(None, "rep", "acct"),
    ) + (P(),) * 9
    return jax.shard_map(
        per_device, mesh=mesh, in_specs=placed, out_specs=P("rep", "acct", None), check_vma=False
    )
```

```python
import functools

import jax
import jax.numpy as jnp
from jax import lax
from jax.experimental import pallas as pl
from jax.experimental.pallas import tpu as pltpu
from jax.sharding import PartitionSpec as P

NB = 3
NZ, NX, NC, NR = 8, 4, 2, 4
BD, TD, ROWS, D = 8, 32, 32, 512
PARTS = 1
PR = ROWS // PARTS
SLOTS = 16
CAP = 2 * SLOTS
COL = NZ * BD
EARLY = COL + (NX - 1) * SLOTS
BF, F32, I32 = jnp.bfloat16, jnp.float32, jnp.int32

SMEM = pl.BlockSpec(memory_space=pltpu.SMEM)
VMEM = pl.BlockSpec(memory_space=pltpu.VMEM)


def call(kernel, name, outs, specs, args, scratch=()):
    many = isinstance(outs, list)
    return pl.pallas_call(
        kernel,
        out_shape=outs,
        in_specs=specs,
        out_specs=[VMEM] * len(outs) if many else VMEM,
        scratch_shapes=scratch,
        compiler_params=pltpu.CompilerParams(vmem_limit_bytes=14 << 20),
        name=name,
    )(*args)


def shape(*dims, dtype=BF):
    return jax.ShapeDtypeStruct(dims, dtype)


def z_shift(s):
    n = NX * NC
    return [(i, ((i // n + s) % NZ) * n + i % n) for i in range(NZ * n)]


def x_shift(s):
    n = NX * NC
    return [(i, (i // n) * n + ((i // NC + s) % NX) * NC + i % NC) for i in range(NZ * n)]


def core_swap():
    return [(i, i ^ 1) for i in range(NZ * NX * NC)]


def rep_shift(s):
    return [(i, (i + s) % NR) for i in range(NR)]


def early_block(place, column, lanes):
    block = column[jnp.clip(place, 0, COL - 1)]
    for d, lane in enumerate(lanes):
        low = COL + d * SLOTS
        slot = jnp.clip(place - low, 0, SLOTS - 1)
        block = jnp.where((place >= low) & (place < low + SLOTS), lane[slot], block)
    return block


def late_block(place, late, put):
    for d, lane in enumerate(late):
        low = EARLY + d * SLOTS

        @pl.when((place >= low) & (place < low + SLOTS))
        def _(lane=lane, low=low):
            put(lane[place - low])


def gather_kernel(batch, base, n_column, idx_ref, *refs):
    pieces, outs = refs[:n_column], refs[n_column:]
    if n_column > 1:
        column, lanes = outs[0], outs[1:]
        low = 0
        for piece in pieces:
            column[low : low + piece.shape[0]] = piece[...]
            low += piece.shape[0]
    else:
        column, lanes = pieces[0], outs
    for s in range(SLOTS):
        for d, lane in enumerate(lanes):
            lane[s] = column[idx_ref[batch, d * CAP + base + s]]


def gather_call(batch, base, idx, pieces):
    outs = [shape(COL, PR, D)] if len(pieces) > 1 else []
    return call(
        functools.partial(gather_kernel, batch, base, len(pieces)),
        "gather",
        outs + [shape(SLOTS, PR, D)] * (NX - 1),
        [SMEM] + [VMEM] * len(pieces),
        (idx, *pieces),
    )


def swap_kernel(batch, idx_ref, more_ref, column, *refs):
    lanes, late, out = refs[: NX - 1], refs[NX - 1 : -1], refs[-1]
    for t in range(TD):
        out[t] = early_block(idx_ref[batch, t], column, lanes)

    @pl.when(more_ref[batch] == 1)
    def _():
        def body(t, carry):
            def put(block):
                out[t] = block

            late_block(idx_ref[batch, t], late, put)
            return carry

        lax.fori_loop(0, TD, body, 0)


def swap_call(batch, idx, more, table):
    return call(
        functools.partial(swap_kernel, batch),
        "swap",
        shape(TD, PR, D),
        [SMEM] * 2 + [VMEM] * len(table),
        (idx, more, *table),
    )


def hidden_of(block, code):
    return jnp.maximum(block.astype(F32) + code, 0.0).astype(BF)


def local_kernel(batch, idx_ref, more_ref, code_ref, column, *refs):
    lanes, late, out = refs[: NX - 1], refs[NX - 1 : -1], refs[-1]
    for t in range(TD):
        block = early_block(idx_ref[batch, t], column, lanes)
        out[t] = hidden_of(block, code_ref[batch, t : t + 1, :])

    @pl.when(more_ref[batch] == 1)
    def _():
        def body(t, carry):
            def put(block):
                out[t] = hidden_of(block, code_ref[batch, pl.ds(t, 1), :])

            late_block(idx_ref[batch, t], late, put)
            return carry

        lax.fori_loop(0, TD, body, 0)


def local_call(batch, idx, more, code, table):
    return call(
        functools.partial(local_kernel, batch),
        "local",
        shape(TD, PR, D),
        [SMEM] * 2 + [VMEM] * (1 + len(table)),
        (idx, more, code, *table),
    )


def message_kernel(batch, idx_ref, code_ref, w2_ref, local_ref, swapped_ref, out_ref, hidden_ref):
    for t in range(TD):
        crossed = hidden_of(swapped_ref[t], code_ref[batch, t : t + 1, :])
        hidden_ref[t] = jnp.where(idx_ref[batch, t] >= 0, local_ref[t], crossed)
    hidden = hidden_ref[...].reshape(TD * PR, D)
    out_ref[...] = jnp.dot(hidden, w2_ref[...], preferred_element_type=F32).astype(BF)


def message_call(batch, idx, code, w2, local, swapped):
    return call(
        functools.partial(message_kernel, batch),
        "message",
        shape(TD * PR, D),
        [SMEM] + [VMEM] * 4,
        (idx, code, w2, local, swapped),
        [pltpu.VMEM((TD, PR, D), BF)],
    )


def sum_kernel(lhs_ref, *refs):
    messages, outs = refs[:PARTS], refs[PARTS:]
    n, depth = BD * PR, TD * PR
    agg = 0.0
    for p, message in enumerate(messages):
        lhs = lhs_ref[:, p * depth : (p + 1) * depth]
        agg = agg + jnp.dot(lhs, message[...], preferred_element_type=F32)
    outs[0][...] = agg[:n]
    for j in range(1, NR):
        outs[j][...] = agg[j * n : (j + 1) * n].astype(BF)


def sum_call(lhs, messages):
    n = BD * PR
    return call(
        sum_kernel,
        "sum",
        [shape(n, D, dtype=F32)] + [shape(n, D)] * (NR - 1),
        [VMEM] * (1 + PARTS),
        (lhs, *messages),
    )


def prepare_kernel(rep_ref, masks_ref, dst_ref, *outs):
    mask_ref = outs[-1]
    outs = outs[:-1]
    depth = TD * PR
    tile = lax.broadcasted_iota(I32, (TD, depth), 0)
    place = lax.broadcasted_iota(I32, (TD, depth), 1)
    spread = ((place >= tile * PR) & (place < (tile + 1) * PR)).astype(BF)
    block = lax.broadcasted_iota(I32, (BD, TD), 0)
    rep = rep_ref[0]
    for batch in range(NB):
        hot = (dst_ref[batch : batch + 1, :] == block).astype(BF)
        hot = jnp.dot(hot, spread, preferred_element_type=F32).astype(BF)
        for p in range(PARTS):
            bits = masks_ref[batch, :, p * PR : (p + 1) * PR, :].astype(F32)
            mask_ref[:, p * depth : (p + 1) * depth] = bits.reshape(depth, NR * ROWS).T.astype(BF)
        for j in range(NR):
            r = lax.rem(rep + j, NR)
            for q in range(PARTS):
                rows = mask_ref[pl.ds(pl.multiple_of(r * ROWS + q * PR, PR), PR), :]
                for k in range(BD):
                    low = (j * BD + k) * PR
                    for p in range(PARTS):
                        part = rows[:, p * depth : (p + 1) * depth]
                        outs[batch * PARTS + q][low : low + PR, p * depth : (p + 1) * depth] = part * hot[k : k + 1, :]


def prepare_call(rep, masks, dst):
    return call(
        prepare_kernel,
        "prepare",
        [shape(NR * BD * PR, TD * ROWS)] * (NB * PARTS),
        [SMEM] + [VMEM] * 2,
        (rep, masks, dst),
        [pltpu.VMEM((NR * ROWS, TD * ROWS), BF)],
    )


def sigmoid(v):
    return 0.5 * jnp.tanh(0.5 * v) + 0.5


def update_kernel(batch, part, last, own, in1, in2, in3, state, member, gain, w_in, w_hid, b_in, b_hid, w1, *outs):
    total = own[...] + in1[...].astype(F32) + in2[...].astype(F32) + in3[...].astype(F32)
    mean = jnp.mean(total, axis=-1, keepdims=True)
    centred = total - mean
    var = jnp.mean(centred * centred, axis=-1, keepdims=True)
    x = (centred * lax.rsqrt(var + 1e-05) * gain[...]).astype(BF)
    old = state[...]
    gin = jnp.dot(x, w_in[...], preferred_element_type=F32) + b_in[...]
    ghid = jnp.dot(old, w_hid[...], preferred_element_type=F32) + b_hid[...]
    z = sigmoid(gin[:, :D] + ghid[:, :D])
    r = sigmoid(gin[:, D : 2 * D] + ghid[:, D : 2 * D])
    cand = jnp.tanh(gin[:, 2 * D :] + r * ghid[:, 2 * D :])
    fresh = (1.0 - z) * cand + z * old.astype(F32)
    new = jnp.where(member[batch, part] == 1, fresh, old.astype(F32)).astype(BF)
    outs[0][...] = new
    if not last:
        outs[1][...] = jnp.dot(new, w1[...], preferred_element_type=F32).astype(BF)


def update_call(batch, part, last, *args):
    return call(
        functools.partial(update_kernel, batch, part, last),
        "update",
        [shape(BD * PR, D)] * (1 if last else 2),
        [VMEM] * len(args),
        args,
    )


def first_kernel(state_ref, w1, *outs):
    for p in range(PARTS):
        state = state_ref[:, p * PR : (p + 1) * PR, :].reshape(BD * PR, D)
        outs[p][...] = jnp.dot(state, w1[...], preferred_element_type=F32).astype(BF)
        outs[PARTS + p][...] = state


def first_call(state, w1):
    return call(first_kernel, "first", [shape(BD * PR, D)] * (2 * PARTS), [VMEM] * 2, (state, w1))


def ranks(dev, loc):
    tile = jnp.arange(NC * TD, dtype=I32)
    before = tile[None, :] < tile[:, None]
    pair = dev % (NX * NC)
    lane = pair[..., :, None] == pair[..., None, :]
    block = dev * BD + loc
    same = block[..., :, None] == block[..., None, :]
    first = ~jnp.any(same & before, axis=-1)
    new = jnp.where(before & lane & first[..., None, :], 1, 0)
    rank = jnp.sum(new, axis=-1)
    home = jnp.sum(jnp.where(same & first[..., None, :], rank[..., None, :], 0), axis=-1)
    return home


def places(src_dev, src_local):
    me = lax.axis_index("acct")
    z, x, c = me // (NX * NC), (me // NC) % NX, me % NC
    dev = src_dev.reshape(NB, NZ, NX, NC * TD)
    loc = src_local.reshape(NB, NZ, NX, NC * TD)
    away = (dev // NC) % NX != jnp.arange(NX, dtype=I32)[None, None, :, None]
    deepest = jnp.max(jnp.where(away, ranks(dev, loc), 0), axis=(1, 2, 3))
    dev = lax.dynamic_slice_in_dim(dev, z, 1, 1)[:, 0]
    loc = lax.dynamic_slice_in_dim(loc, z, 1, 1)[:, 0]
    sz, sx, sc = dev // (NX * NC), (dev // NC) % NX, dev % NC
    column = ((sz - z) % NZ) * BD + loc
    rank = ranks(dev, loc)
    mine = sx * NC + sc == x * NC + c
    slots = jnp.arange(CAP, dtype=I32)
    chosen = mine[:, :, None, :] & (rank[:, :, None, :] == slots[None, None, :, None])
    out = jnp.max(jnp.where(chosen, column[:, :, None, :], 0), axis=-1)
    lanes = (x + jnp.arange(1, NX, dtype=I32)) % NX
    turn = (lanes[:, None] == jnp.arange(NX, dtype=I32)[None, :]).astype(I32)
    send = jnp.sum(out[:, None, :, :] * turn[None, :, :, None], axis=2).reshape(NB, -1)
    here = (jnp.arange(NX, dtype=I32) == x).astype(I32)[None, :, None]
    column, rank, sx, sc = (jnp.sum(a * here, axis=1) for a in (column, rank, sx, sc))
    lane = (sx - x) % NX
    early = COL + (lane - 1) * SLOTS + rank
    place = jnp.where(rank < SLOTS, early, early + (NX - 2) * SLOTS)
    place = jnp.where(lane == 0, column, place).reshape(NB, NC, TD)
    local = (sc == c).reshape(NB, NC, TD)
    self_ = (jnp.arange(NC, dtype=I32) == c).astype(I32)[None, :, None]
    final = jnp.sum(jnp.where(local, place, -1) * self_, axis=1)
    swap = jnp.sum(jnp.where(local, place, 0) * (1 - self_), axis=1)
    return send, swap, final, (deepest >= SLOTS).astype(I32)


def along_x(lanes):
    order = [2, 1, 3]
    got = {d: lax.ppermute(lanes[d - 1], "acct", x_shift(d)) for d in order}
    return [got[d] for d in range(NX - 1, 0, -1)]


def along_z(pre):
    up, down = [pre], [pre]
    for step in range(3):
        up.append(lax.ppermute(up[-1], "acct", z_shift(1)))
        down.append(lax.ppermute(down[-1], "acct", z_shift(-1)))
    half = BD // 2
    far_up = lax.ppermute(up[3][:half], "acct", z_shift(1))
    far_down = lax.ppermute(down[3][half:], "acct", z_shift(-1))
    return [pre, down[1], down[2], down[3], far_up, far_down, up[3], up[2], up[1]]


def messages_of(batch, pre, send, swap, final, more, code, w2):
    column, *lanes = gather_call(batch, 0, send, along_z(pre.reshape(BD, PR, D)))
    early = along_x(lanes)
    late = lax.cond(
        more[batch] == 1,
        lambda: along_x(gather_call(batch, SLOTS, send, [column])),
        lambda: [jnp.zeros((SLOTS, PR, D), BF)] * (NX - 1),
    )
    table = [column, *early, *late]
    swapped = lax.ppermute(swap_call(batch, swap, more, table), "acct", core_swap())
    local = local_call(batch, final, more, code, table)
    return message_call(batch, final, code, w2, local, swapped)


def per_device(
    memory, src_dev, src_local, dst_local, delta_t, masks, member,
    w_msg1, b_msg1, omega, w_msg2, ln_gain, w_in, w_hid, b_in, b_hid,
):
    rep = lax.axis_index("rep").reshape(1).astype(I32)
    first = first_call(jnp.swapaxes(memory, 0, 1), w_msg1)
    pre, state = first[:PARTS], first[PARTS:]
    send, swap, final, more = places(src_dev, src_local)
    code = jnp.cos(delta_t[:, :, None] * omega) + b_msg1
    lhs = prepare_call(rep, masks, dst_local)
    chosen = jnp.transpose(member.reshape(NB, PARTS, PR, BD), (0, 1, 3, 2)).reshape(NB, PARTS, BD * PR, 1)
    for batch in range(NB):
        last = batch == NB - 1
        messages = [messages_of(batch, p, send, swap, final, more, code, w_msg2) for p in pre]
        sums = [sum_call(lhs[batch * PARTS + q], messages) for q in range(PARTS)]
        results = []
        for q in range(PARTS):
            own, *shares = sums[q]
            got = {j: lax.ppermute(shares[j - 1], "rep", rep_shift(j)) for j in (2, 1, 3)}
            results.append(
                update_call(
                    batch, q, last, own, got[1], got[2], got[3], state[q], chosen, ln_gain[None],
                    w_in, w_hid, b_in[None], b_hid[None], w_msg1,
                )
            )
        state = [r[0] for r in results]
        pre = [r[-1] for r in results]
    whole = jnp.concatenate([s.reshape(BD, PR, D) for s in state], axis=1)
    return jnp.swapaxes(whole, 0, 1)


def solution(mesh):
    placed = (
        P("rep", "acct", None),
        P(),
        P(),
        P(None, "acct"),
        P(None, "acct"),
        P(None, "acct", "rep", None),
        P(None, "rep", "acct"),
    ) + (P(),) * 9
    return jax.shard_map(
        per_device, mesh=mesh, in_specs=placed, out_specs=P("rep", "acct", None), check_vma=False
    )
```

```python
import functools

import jax
import jax.numpy as jnp
from jax import lax
from jax.experimental import pallas as pl
from jax.experimental.pallas import tpu as pltpu
from jax.sharding import PartitionSpec as P

NB = 3
NZ, NX, NC, NR = 8, 4, 2, 4
BD, TD, ROWS, D = 8, 32, 32, 512
PARTS = 1
PR = ROWS // PARTS
SLOTS = 16
CAP = 2 * SLOTS
COL = NZ * BD
EARLY = COL + (NX - 1) * SLOTS
BF, F32, I32 = jnp.bfloat16, jnp.float32, jnp.int32

ANY = pl.BlockSpec(memory_space=pl.ANY)
SMEM = pl.BlockSpec(memory_space=pltpu.SMEM)
VMEM = pl.BlockSpec(memory_space=pltpu.VMEM)


def call(kernel, name, outs, specs, args, scratch=()):
    many = isinstance(outs, list)
    return pl.pallas_call(
        kernel,
        out_shape=outs,
        in_specs=specs,
        out_specs=[VMEM] * len(outs) if many else VMEM,
        scratch_shapes=scratch,
        compiler_params=pltpu.CompilerParams(vmem_limit_bytes=14 << 20),
        name=name,
    )(*args)


def shape(*dims, dtype=BF):
    return jax.ShapeDtypeStruct(dims, dtype)


def z_shift(s):
    n = NX * NC
    return [(i, ((i // n + s) % NZ) * n + i % n) for i in range(NZ * n)]


def x_shift(s):
    n = NX * NC
    return [(i, (i // n) * n + ((i // NC + s) % NX) * NC + i % NC) for i in range(NZ * n)]


def core_swap():
    return [(i, i ^ 1) for i in range(NZ * NX * NC)]


def rep_shift(s):
    return [(i, (i + s) % NR) for i in range(NR)]


def early_block(place, column, lanes):
    block = column[jnp.clip(place, 0, COL - 1)]
    for d, lane in enumerate(lanes):
        low = COL + d * SLOTS
        slot = jnp.clip(place - low, 0, SLOTS - 1)
        block = jnp.where((place >= low) & (place < low + SLOTS), lane[slot], block)
    return block


def late_block(place, late, dst):
    for d, lane in enumerate(late):
        low = EARLY + d * SLOTS

        @pl.when((place >= low) & (place < low + SLOTS))
        def _(lane=lane, low=low):
            pltpu.sync_copy(lane.at[place - low], dst)


def gather_kernel(batch, idx_ref, *refs):
    pieces, column, lanes = refs[: -2 * NX + 1], refs[-2 * NX + 1], refs[-2 * NX + 2 :]
    low = 0
    for piece in pieces:
        column[low : low + piece.shape[0]] = piece[...]
        low += piece.shape[0]
    for s in range(SLOTS):
        for n, lane in enumerate(lanes):
            late, d = divmod(n, NX - 1)
            lane[s] = column[idx_ref[batch, d * CAP + late * SLOTS + s]]


def gather_call(batch, idx, pieces):
    return call(
        functools.partial(gather_kernel, batch),
        "gather",
        [shape(COL, PR, D)] + [shape(SLOTS, PR, D)] * (2 * NX - 2),
        [SMEM] + [VMEM] * len(pieces),
        (idx, *pieces),
    )


def swap_kernel(batch, idx_ref, more_ref, column, *refs):
    lanes, late, out = refs[: NX - 1], refs[NX - 1 : -1], refs[-1]
    for t in range(TD):
        out[t] = early_block(idx_ref[batch, t], column, lanes)

    @pl.when(more_ref[batch] == 1)
    def _():
        def body(t, carry):
            late_block(idx_ref[batch, t], late, out.at[t])
            return carry

        lax.fori_loop(0, TD, body, 0)


def swap_call(batch, idx, more, table):
    return call(
        functools.partial(swap_kernel, batch),
        "swap",
        shape(TD, PR, D),
        [SMEM] * 2 + [VMEM] * NX + [ANY] * (NX - 1),
        (idx, more, *table),
    )


def hidden_of(block, code):
    return jnp.maximum(block.astype(F32) + code, 0.0).astype(BF)


def local_kernel(batch, idx_ref, more_ref, code_ref, column, *refs):
    lanes, late, out, held = refs[: NX - 1], refs[NX - 1 : -2], refs[-2], refs[-1]
    for t in range(TD):
        block = early_block(idx_ref[batch, t], column, lanes)
        out[t] = hidden_of(block, code_ref[batch, t : t + 1, :])

    @pl.when(more_ref[batch] == 1)
    def _():
        def body(t, carry):
            place = idx_ref[batch, t]
            late_block(place, late, held)

            @pl.when(place >= EARLY)
            def _():
                out[t] = hidden_of(held[...], code_ref[batch, pl.ds(t, 1), :])

            return carry

        lax.fori_loop(0, TD, body, 0)


def local_call(batch, idx, more, code, table):
    return call(
        functools.partial(local_kernel, batch),
        "local",
        shape(TD, PR, D),
        [SMEM] * 2 + [VMEM] * (1 + NX) + [ANY] * (NX - 1),
        (idx, more, code, *table),
        [pltpu.VMEM((PR, D), BF)],
    )


def message_kernel(batch, idx_ref, code_ref, w2_ref, local_ref, swapped_ref, out_ref, hidden_ref):
    for t in range(TD):
        crossed = hidden_of(swapped_ref[t], code_ref[batch, t : t + 1, :])
        hidden_ref[t] = jnp.where(idx_ref[batch, t] >= 0, local_ref[t], crossed)
    hidden = hidden_ref[...].reshape(TD * PR, D)
    out_ref[...] = jnp.dot(hidden, w2_ref[...], preferred_element_type=F32).astype(BF)


def message_call(batch, idx, code, w2, local, swapped):
    return call(
        functools.partial(message_kernel, batch),
        "message",
        shape(TD * PR, D),
        [SMEM] + [VMEM] * 4,
        (idx, code, w2, local, swapped),
        [pltpu.VMEM((TD, PR, D), BF)],
    )


def sum_kernel(lhs_ref, *refs):
    messages, outs = refs[:PARTS], refs[PARTS:]
    n, depth = BD * PR, TD * PR
    agg = 0.0
    for p, message in enumerate(messages):
        lhs = lhs_ref[:, p * depth : (p + 1) * depth]
        agg = agg + jnp.dot(lhs, message[...], preferred_element_type=F32)
    outs[0][...] = agg[:n]
    for j in range(1, NR):
        outs[j][...] = agg[j * n : (j + 1) * n].astype(BF)


def sum_call(lhs, messages):
    n = BD * PR
    return call(
        sum_kernel,
        "sum",
        [shape(n, D, dtype=F32)] + [shape(n, D)] * (NR - 1),
        [VMEM] * (1 + PARTS),
        (lhs, *messages),
    )


def prepare_kernel(rep_ref, masks_ref, dst_ref, *outs):
    mask_ref = outs[-1]
    outs = outs[:-1]
    depth = TD * PR
    tile = lax.broadcasted_iota(I32, (TD, depth), 0)
    place = lax.broadcasted_iota(I32, (TD, depth), 1)
    spread = ((place >= tile * PR) & (place < (tile + 1) * PR)).astype(BF)
    block = lax.broadcasted_iota(I32, (BD, TD), 0)
    rep = rep_ref[0]
    for batch in range(NB):
        hot = (dst_ref[batch : batch + 1, :] == block).astype(BF)
        hot = jnp.dot(hot, spread, preferred_element_type=F32).astype(BF)
        for p in range(PARTS):
            bits = masks_ref[batch, :, p * PR : (p + 1) * PR, :].astype(F32)
            mask_ref[:, p * depth : (p + 1) * depth] = bits.reshape(depth, NR * ROWS).T.astype(BF)
        for j in range(NR):
            r = lax.rem(rep + j, NR)
            for q in range(PARTS):
                rows = mask_ref[pl.ds(pl.multiple_of(r * ROWS + q * PR, PR), PR), :]
                for k in range(BD):
                    low = (j * BD + k) * PR
                    for p in range(PARTS):
                        part = rows[:, p * depth : (p + 1) * depth]
                        outs[batch * PARTS + q][low : low + PR, p * depth : (p + 1) * depth] = part * hot[k : k + 1, :]


def prepare_call(rep, masks, dst):
    return call(
        prepare_kernel,
        "prepare",
        [shape(NR * BD * PR, TD * ROWS)] * (NB * PARTS),
        [SMEM] + [VMEM] * 2,
        (rep, masks, dst),
        [pltpu.VMEM((NR * ROWS, TD * ROWS), BF)],
    )


def sigmoid(v):
    return 0.5 * jnp.tanh(0.5 * v) + 0.5


def update_kernel(batch, part, last, own, in1, in2, in3, state, member, gain, w_in, w_hid, b_in, b_hid, w1, *outs):
    total = own[...] + in1[...].astype(F32) + in2[...].astype(F32) + in3[...].astype(F32)
    mean = jnp.mean(total, axis=-1, keepdims=True)
    centred = total - mean
    var = jnp.mean(centred * centred, axis=-1, keepdims=True)
    x = (centred * lax.rsqrt(var + 1e-05) * gain[...]).astype(BF)
    old = state[...]
    gin = jnp.dot(x, w_in[...], preferred_element_type=F32) + b_in[...]
    ghid = jnp.dot(old, w_hid[...], preferred_element_type=F32) + b_hid[...]
    z = sigmoid(gin[:, :D] + ghid[:, :D])
    r = sigmoid(gin[:, D : 2 * D] + ghid[:, D : 2 * D])
    cand = jnp.tanh(gin[:, 2 * D :] + r * ghid[:, 2 * D :])
    fresh = (1.0 - z) * cand + z * old.astype(F32)
    new = jnp.where(member[batch, part] == 1, fresh, old.astype(F32)).astype(BF)
    outs[0][...] = new
    if not last:
        outs[1][...] = jnp.dot(new, w1[...], preferred_element_type=F32).astype(BF)


def update_call(batch, part, last, *args):
    return call(
        functools.partial(update_kernel, batch, part, last),
        "update",
        [shape(BD * PR, D)] * (1 if last else 2),
        [VMEM] * len(args),
        args,
    )


def first_kernel(state_ref, w1, *outs):
    for p in range(PARTS):
        state = state_ref[:, p * PR : (p + 1) * PR, :].reshape(BD * PR, D)
        outs[p][...] = jnp.dot(state, w1[...], preferred_element_type=F32).astype(BF)
        outs[PARTS + p][...] = state


def first_call(state, w1):
    return call(first_kernel, "first", [shape(BD * PR, D)] * (2 * PARTS), [VMEM] * 2, (state, w1))


def ranks(dev, loc):
    tile = jnp.arange(NC * TD, dtype=I32)
    before = tile[None, :] < tile[:, None]
    pair = dev % (NX * NC)
    lane = pair[..., :, None] == pair[..., None, :]
    block = dev * BD + loc
    same = block[..., :, None] == block[..., None, :]
    first = ~jnp.any(same & before, axis=-1)
    new = jnp.where(before & lane & first[..., None, :], 1, 0)
    rank = jnp.sum(new, axis=-1)
    home = jnp.sum(jnp.where(same & first[..., None, :], rank[..., None, :], 0), axis=-1)
    return home


def places(src_dev, src_local):
    me = lax.axis_index("acct")
    z, x, c = me // (NX * NC), (me // NC) % NX, me % NC
    dev = src_dev.reshape(NB, NZ, NX, NC * TD)
    loc = src_local.reshape(NB, NZ, NX, NC * TD)
    dev = lax.dynamic_slice_in_dim(dev, z, 1, 1)[:, 0]
    loc = lax.dynamic_slice_in_dim(loc, z, 1, 1)[:, 0]
    sz, sx, sc = dev // (NX * NC), (dev // NC) % NX, dev % NC
    column = ((sz - z) % NZ) * BD + loc
    rank = ranks(dev, loc)
    mine = sx * NC + sc == x * NC + c
    slots = jnp.arange(CAP, dtype=I32)
    chosen = mine[:, :, None, :] & (rank[:, :, None, :] == slots[None, None, :, None])
    out = jnp.max(jnp.where(chosen, column[:, :, None, :], 0), axis=-1)
    lanes = (x + jnp.arange(1, NX, dtype=I32)) % NX
    turn = (lanes[:, None] == jnp.arange(NX, dtype=I32)[None, :]).astype(I32)
    send = jnp.sum(out[:, None, :, :] * turn[None, :, :, None], axis=2).reshape(NB, -1)
    here = (jnp.arange(NX, dtype=I32) == x).astype(I32)[None, :, None]
    column, rank, sx, sc = (jnp.sum(a * here, axis=1) for a in (column, rank, sx, sc))
    lane = (sx - x) % NX
    early = COL + (lane - 1) * SLOTS + rank
    place = jnp.where(rank < SLOTS, early, early + (NX - 2) * SLOTS)
    place = jnp.where(lane == 0, column, place).reshape(NB, NC, TD)
    local = (sc == c).reshape(NB, NC, TD)
    self_ = (jnp.arange(NC, dtype=I32) == c).astype(I32)[None, :, None]
    final = jnp.sum(jnp.where(local, place, -1) * self_, axis=1)
    swap = jnp.sum(jnp.where(local, place, 0) * (1 - self_), axis=1)
    return send, swap, final


def second_round(src_dev, src_local):
    dev = src_dev.reshape(NB, NZ, NX, NC * TD)
    loc = src_local.reshape(NB, NZ, NX, NC * TD)
    away = (dev // NC) % NX != jnp.arange(NX, dtype=I32)[None, None, :, None]
    deepest = jnp.max(jnp.where(away, ranks(dev, loc), 0), axis=(1, 2, 3))
    return (deepest >= SLOTS).astype(I32)


def along_x(lanes):
    order = [2, 1, 3]
    got = {d: lax.ppermute(lanes[d - 1], "acct", x_shift(d)) for d in order}
    return [got[d] for d in range(NX - 1, 0, -1)]


def along_z(pre):
    up, down = [pre], [pre]
    for step in range(3):
        up.append(lax.ppermute(up[-1], "acct", z_shift(1)))
        down.append(lax.ppermute(down[-1], "acct", z_shift(-1)))
    half = BD // 2
    far_up = lax.ppermute(up[3][:half], "acct", z_shift(1))
    far_down = lax.ppermute(down[3][half:], "acct", z_shift(-1))
    return [pre, down[1], down[2], down[3], far_up, far_down, up[3], up[2], up[1]]


def late_lanes(more, lanes):
    def step(carry):
        return carry[0] - 1, along_x(carry[1])

    return lax.while_loop(lambda carry: carry[0] > 0, step, (more, lanes))[1]


def per_device(
    memory, src_dev, src_local, dst_local, delta_t, masks, member,
    w_msg1, b_msg1, omega, w_msg2, ln_gain, w_in, w_hid, b_in, b_hid,
):
    rep = lax.axis_index("rep").reshape(1).astype(I32)
    first = first_call(jnp.swapaxes(memory, 0, 1), w_msg1)
    pre, state = first[:PARTS], first[PARTS:]
    send, swap, final = places(src_dev, src_local)
    code = jnp.cos(delta_t[:, :, None] * omega) + b_msg1
    lhs = prepare_call(rep, masks, dst_local)
    chosen = jnp.transpose(member.reshape(NB, PARTS, PR, BD), (0, 1, 3, 2)).reshape(NB, PARTS, BD * PR, 1)
    more = None
    for batch in range(NB):
        last = batch == NB - 1
        messages = []
        for p in range(PARTS):
            column, *lanes = gather_call(batch, send, along_z(pre[p].reshape(BD, PR, D)))
            if more is None:
                dev, loc, lanes[0] = lax.optimization_barrier((src_dev, src_local, lanes[0]))
                more = second_round(dev, loc)
            early = along_x(lanes[: NX - 1])
            late = late_lanes(more[batch], lanes[NX - 1 :])
            if batch == 0 and p == 0:
                early, code, lhs = lax.optimization_barrier((early, code, lhs))
            table = [column, *early, *late]
            swapped = lax.ppermute(swap_call(batch, swap, more, table), "acct", core_swap())
            local = local_call(batch, final, more, code, table)
            messages.append(message_call(batch, final, code, w_msg2, local, swapped))
        sums = [sum_call(lhs[batch * PARTS + q], messages) for q in range(PARTS)]
        results = []
        for q in range(PARTS):
            own, *shares = sums[q]
            got = {j: lax.ppermute(shares[j - 1], "rep", rep_shift(j)) for j in (2, 1, 3)}
            results.append(
                update_call(
                    batch, q, last, own, got[1], got[2], got[3], state[q], chosen, ln_gain[None],
                    w_in, w_hid, b_in[None], b_hid[None], w_msg1,
                )
            )
        state = [r[0] for r in results]
        pre = [r[-1] for r in results]
    whole = jnp.concatenate([s.reshape(BD, PR, D) for s in state], axis=1)
    return jnp.swapaxes(whole, 0, 1)


def solution(mesh):
    placed = (
        P("rep", "acct", None),
        P(),
        P(),
        P(None, "acct"),
        P(None, "acct"),
        P(None, "acct", "rep", None),
        P(None, "rep", "acct"),
    ) + (P(),) * 9
    return jax.shard_map(
        per_device, mesh=mesh, in_specs=placed, out_specs=P("rep", "acct", None), check_vma=False
    )
```

```python
import functools

import jax
import jax.numpy as jnp
from jax import lax
from jax.experimental import pallas as pl
from jax.experimental.pallas import tpu as pltpu
from jax.sharding import PartitionSpec as P

NB = 3
NZ, NX, NC, NR = 8, 4, 2, 4
BD, TD, ROWS, D = 8, 32, 32, 512
PARTS = 1
PR = ROWS // PARTS
CAP = 2 * NZ * NC
DEPTHS = (15, 16, CAP)
COL = NZ * BD
BF, F32, I32 = jnp.bfloat16, jnp.float32, jnp.int32

SMEM = pl.BlockSpec(memory_space=pltpu.SMEM)
VMEM = pl.BlockSpec(memory_space=pltpu.VMEM)


def call(kernel, name, outs, specs, args, scratch=()):
    many = isinstance(outs, list)
    return pl.pallas_call(
        kernel,
        out_shape=outs,
        in_specs=specs,
        out_specs=[VMEM] * len(outs) if many else VMEM,
        scratch_shapes=scratch,
        compiler_params=pltpu.CompilerParams(vmem_limit_bytes=14 << 20),
        name=name,
    )(*args)


def shape(*dims, dtype=BF):
    return jax.ShapeDtypeStruct(dims, dtype)


def z_shift(s):
    n = NX * NC
    return [(i, ((i // n + s) % NZ) * n + i % n) for i in range(NZ * n)]


def x_shift(s):
    n = NX * NC
    return [(i, (i // n) * n + ((i // NC + s) % NX) * NC + i % NC) for i in range(NZ * n)]


def core_swap():
    return [(i, i ^ 1) for i in range(NZ * NX * NC)]


def rep_shift(s):
    return [(i, (i + s) % NR) for i in range(NR)]


def block_at(place, column, lanes):
    block = column[jnp.clip(place, 0, COL - 1)]
    for d, lane in enumerate(lanes):
        low = COL + d * CAP
        slot = jnp.clip(place - low, 0, lane.shape[0] - 1)
        block = jnp.where((place >= low) & (place < low + CAP), lane[slot], block)
    return block


def gather_kernel(batch, idx_ref, *refs):
    pieces, column, lanes = refs[:-NX], refs[-NX], refs[-NX + 1 :]
    low = 0
    for piece in pieces:
        column[low : low + piece.shape[0]] = piece[...]
        low += piece.shape[0]
    for s in range(lanes[0].shape[0]):
        for d, lane in enumerate(lanes):
            lane[s] = column[idx_ref[batch, d * CAP + s]]


def gather_call(batch, depth, idx, pieces):
    return call(
        functools.partial(gather_kernel, batch),
        "gather",
        [shape(COL, PR, D)] + [shape(depth, PR, D)] * (NX - 1),
        [SMEM] + [VMEM] * len(pieces),
        (idx, *pieces),
    )


def swap_kernel(batch, idx_ref, column, *refs):
    lanes, out = refs[:-1], refs[-1]
    for t in range(TD):
        out[t] = block_at(idx_ref[batch, t], column, lanes)


def swap_call(batch, idx, table):
    return call(
        functools.partial(swap_kernel, batch),
        "swap",
        shape(TD, PR, D),
        [SMEM] + [VMEM] * NX,
        (idx, *table),
    )


def hidden_of(block, code):
    return jnp.maximum(block.astype(F32) + code, 0.0).astype(BF)


def local_kernel(batch, idx_ref, code_ref, column, *refs):
    lanes, out = refs[:-1], refs[-1]
    for t in range(TD):
        block = block_at(idx_ref[batch, t], column, lanes)
        out[t] = hidden_of(block, code_ref[batch, t : t + 1, :])


def local_call(batch, idx, code, table):
    return call(
        functools.partial(local_kernel, batch),
        "local",
        shape(TD, PR, D),
        [SMEM] + [VMEM] * (1 + NX),
        (idx, code, *table),
    )


def message_kernel(batch, idx_ref, code_ref, w2_ref, local_ref, swapped_ref, out_ref, hidden_ref):
    for t in range(TD):
        crossed = hidden_of(swapped_ref[t], code_ref[batch, t : t + 1, :])
        hidden_ref[t] = jnp.where(idx_ref[batch, t] >= 0, local_ref[t], crossed)
    hidden = hidden_ref[...].reshape(TD * PR, D)
    out_ref[...] = jnp.dot(hidden, w2_ref[...], preferred_element_type=F32).astype(BF)


def message_call(batch, idx, code, w2, local, swapped):
    return call(
        functools.partial(message_kernel, batch),
        "message",
        shape(TD * PR, D),
        [SMEM] + [VMEM] * 4,
        (idx, code, w2, local, swapped),
        [pltpu.VMEM((TD, PR, D), BF)],
    )


def sum_kernel(lhs_ref, *refs):
    messages, outs = refs[:PARTS], refs[PARTS:]
    n, depth = BD * PR, TD * PR
    agg = 0.0
    for p, message in enumerate(messages):
        lhs = lhs_ref[:, p * depth : (p + 1) * depth]
        agg = agg + jnp.dot(lhs, message[...], preferred_element_type=F32)
    outs[0][...] = agg[:n]
    for j in range(1, NR):
        outs[j][...] = agg[j * n : (j + 1) * n].astype(BF)


def sum_call(lhs, messages):
    n = BD * PR
    return call(
        sum_kernel,
        "sum",
        [shape(n, D, dtype=F32)] + [shape(n, D)] * (NR - 1),
        [VMEM] * (1 + PARTS),
        (lhs, *messages),
    )


def prepare_kernel(rep_ref, masks_ref, dst_ref, *outs):
    mask_ref = outs[-1]
    outs = outs[:-1]
    depth = TD * PR
    tile = lax.broadcasted_iota(I32, (TD, depth), 0)
    place = lax.broadcasted_iota(I32, (TD, depth), 1)
    spread = ((place >= tile * PR) & (place < (tile + 1) * PR)).astype(BF)
    block = lax.broadcasted_iota(I32, (BD, TD), 0)
    rep = rep_ref[0]
    for batch in range(NB):
        hot = (dst_ref[batch : batch + 1, :] == block).astype(BF)
        hot = jnp.dot(hot, spread, preferred_element_type=F32).astype(BF)
        for p in range(PARTS):
            bits = masks_ref[batch, :, p * PR : (p + 1) * PR, :].astype(F32)
            mask_ref[:, p * depth : (p + 1) * depth] = bits.reshape(depth, NR * ROWS).T.astype(BF)
        for j in range(NR):
            r = lax.rem(rep + j, NR)
            for q in range(PARTS):
                rows = mask_ref[pl.ds(pl.multiple_of(r * ROWS + q * PR, PR), PR), :]
                for k in range(BD):
                    low = (j * BD + k) * PR
                    for p in range(PARTS):
                        part = rows[:, p * depth : (p + 1) * depth]
                        outs[batch * PARTS + q][low : low + PR, p * depth : (p + 1) * depth] = part * hot[k : k + 1, :]


def prepare_call(rep, masks, dst):
    return call(
        prepare_kernel,
        "prepare",
        [shape(NR * BD * PR, TD * ROWS)] * (NB * PARTS),
        [SMEM] + [VMEM] * 2,
        (rep, masks, dst),
        [pltpu.VMEM((NR * ROWS, TD * ROWS), BF)],
    )


def sigmoid(v):
    return 0.5 * jnp.tanh(0.5 * v) + 0.5


def update_kernel(batch, part, last, own, in1, in2, in3, state, member, gain, w_in, w_hid, b_in, b_hid, w1, *outs):
    total = own[...] + in1[...].astype(F32) + in2[...].astype(F32) + in3[...].astype(F32)
    mean = jnp.mean(total, axis=-1, keepdims=True)
    centred = total - mean
    var = jnp.mean(centred * centred, axis=-1, keepdims=True)
    x = (centred * lax.rsqrt(var + 1e-05) * gain[...]).astype(BF)
    old = state[...]
    gin = jnp.dot(x, w_in[...], preferred_element_type=F32) + b_in[...]
    ghid = jnp.dot(old, w_hid[...], preferred_element_type=F32) + b_hid[...]
    z = sigmoid(gin[:, :D] + ghid[:, :D])
    r = sigmoid(gin[:, D : 2 * D] + ghid[:, D : 2 * D])
    cand = jnp.tanh(gin[:, 2 * D :] + r * ghid[:, 2 * D :])
    fresh = (1.0 - z) * cand + z * old.astype(F32)
    new = jnp.where(member[batch, part] == 1, fresh, old.astype(F32)).astype(BF)
    outs[0][...] = new
    if not last:
        outs[1][...] = jnp.dot(new, w1[...], preferred_element_type=F32).astype(BF)


def update_call(batch, part, last, *args):
    return call(
        functools.partial(update_kernel, batch, part, last),
        "update",
        [shape(BD * PR, D)] * (1 if last else 2),
        [VMEM] * len(args),
        args,
    )


def first_kernel(state_ref, w1, *outs):
    for p in range(PARTS):
        state = state_ref[:, p * PR : (p + 1) * PR, :].reshape(BD * PR, D)
        outs[p][...] = jnp.dot(state, w1[...], preferred_element_type=F32).astype(BF)
        outs[PARTS + p][...] = state


def first_call(state, w1):
    return call(first_kernel, "first", [shape(BD * PR, D)] * (2 * PARTS), [VMEM] * 2, (state, w1))


def ranks(dev, loc):
    tile = jnp.arange(NC * TD, dtype=I32)
    before = tile[None, :] < tile[:, None]
    pair = dev % (NX * NC)
    lane = pair[..., :, None] == pair[..., None, :]
    block = dev * BD + loc
    same = block[..., :, None] == block[..., None, :]
    first = ~jnp.any(same & before, axis=-1)
    new = jnp.where(before & lane & first[..., None, :], 1, 0)
    rank = jnp.sum(new, axis=-1)
    home = jnp.sum(jnp.where(same & first[..., None, :], rank[..., None, :], 0), axis=-1)
    return home


def places(src_dev, src_local):
    me = lax.axis_index("acct")
    z, x, c = me // (NX * NC), (me // NC) % NX, me % NC
    dev = src_dev.reshape(NB, NZ, NX, NC * TD)
    loc = src_local.reshape(NB, NZ, NX, NC * TD)
    dev = lax.dynamic_slice_in_dim(dev, z, 1, 1)[:, 0]
    loc = lax.dynamic_slice_in_dim(loc, z, 1, 1)[:, 0]
    sz, sx, sc = dev // (NX * NC), (dev // NC) % NX, dev % NC
    column = ((sz - z) % NZ) * BD + loc
    rank = ranks(dev, loc)
    mine = sx * NC + sc == x * NC + c
    slots = jnp.arange(CAP, dtype=I32)
    chosen = mine[:, :, None, :] & (rank[:, :, None, :] == slots[None, None, :, None])
    out = jnp.max(jnp.where(chosen, column[:, :, None, :], 0), axis=-1)
    lanes = (x + jnp.arange(1, NX, dtype=I32)) % NX
    turn = (lanes[:, None] == jnp.arange(NX, dtype=I32)[None, :]).astype(I32)
    send = jnp.sum(out[:, None, :, :] * turn[None, :, :, None], axis=2).reshape(NB, -1)
    here = (jnp.arange(NX, dtype=I32) == x).astype(I32)[None, :, None]
    column, rank, sx, sc = (jnp.sum(a * here, axis=1) for a in (column, rank, sx, sc))
    lane = (sx - x) % NX
    place = jnp.where(lane == 0, column, COL + (lane - 1) * CAP + rank).reshape(NB, NC, TD)
    local = (sc == c).reshape(NB, NC, TD)
    self_ = (jnp.arange(NC, dtype=I32) == c).astype(I32)[None, :, None]
    final = jnp.sum(jnp.where(local, place, -1) * self_, axis=1)
    swap = jnp.sum(jnp.where(local, place, 0) * (1 - self_), axis=1)
    return send, swap, final


def depth_class(src_dev, src_local):
    dev = src_dev.reshape(NB, NZ, NX, NC * TD)
    loc = src_local.reshape(NB, NZ, NX, NC * TD)
    away = (dev // NC) % NX != jnp.arange(NX, dtype=I32)[None, None, :, None]
    deepest = jnp.max(jnp.where(away, ranks(dev, loc), 0)) + 1
    return sum((deepest > depth).astype(I32) for depth in DEPTHS[:-1])


def along_x(lanes):
    order = [2, 1, 3]
    got = {d: lax.ppermute(lanes[d - 1], "acct", x_shift(d)) for d in order}
    return [got[d] for d in range(NX - 1, 0, -1)]


def along_z(pre):
    up, down = [pre], [pre]
    for step in range(3):
        up.append(lax.ppermute(up[-1], "acct", z_shift(1)))
        down.append(lax.ppermute(down[-1], "acct", z_shift(-1)))
    half = BD // 2
    far_up = lax.ppermute(up[3][:half], "acct", z_shift(1))
    far_down = lax.ppermute(down[3][half:], "acct", z_shift(-1))
    return [pre, down[1], down[2], down[3], far_up, far_down, up[3], up[2], up[1]]


def per_device(
    memory, src_dev, src_local, dst_local, delta_t, masks, member,
    w_msg1, b_msg1, omega, w_msg2, ln_gain, w_in, w_hid, b_in, b_hid,
):
    rep = lax.axis_index("rep").reshape(1).astype(I32)
    first = first_call(jnp.swapaxes(memory, 0, 1), w_msg1)
    columns = [along_z(p.reshape(BD, PR, D)) for p in first[:PARTS]]
    send, swap, final = places(src_dev, src_local)

    def run(depth, columns, state):
        code = jnp.cos(delta_t[:, :, None] * omega) + b_msg1
        lhs = prepare_call(rep, masks, dst_local)
        chosen = jnp.transpose(member.reshape(NB, PARTS, PR, BD), (0, 1, 3, 2)).reshape(NB, PARTS, BD * PR, 1)
        for batch in range(NB):
            last = batch == NB - 1
            messages = []
            for p in range(PARTS):
                column, *lanes = gather_call(batch, depth, send, columns[p])
                lanes = along_x(lanes)
                if batch == 0 and p == 0:
                    lanes, code, lhs, chosen = lax.optimization_barrier((lanes, code, lhs, chosen))
                table = [column, *lanes]
                swapped = lax.ppermute(swap_call(batch, swap, table), "acct", core_swap())
                local = local_call(batch, final, code, table)
                messages.append(message_call(batch, final, code, w_msg2, local, swapped))
            sums = [sum_call(lhs[batch * PARTS + q], messages) for q in range(PARTS)]
            results = []
            for q in range(PARTS):
                own, *shares = sums[q]
                got = {j: lax.ppermute(shares[j - 1], "rep", rep_shift(j)) for j in (2, 1, 3)}
                results.append(
                    update_call(
                        batch, q, last, own, got[1], got[2], got[3], state[q], chosen, ln_gain[None],
                        w_in, w_hid, b_in[None], b_hid[None], w_msg1,
                    )
                )
            state = [r[0] for r in results]
            if not last:
                columns = [along_z(r[1].reshape(BD, PR, D)) for r in results]
        return state

    branches = [functools.partial(run, depth) for depth in DEPTHS]
    state = lax.switch(depth_class(src_dev, src_local), branches, columns, first[PARTS:])
    whole = jnp.concatenate([s.reshape(BD, PR, D) for s in state], axis=1)
    return jnp.swapaxes(whole, 0, 1)


def solution(mesh):
    placed = (
        P("rep", "acct", None),
        P(),
        P(),
        P(None, "acct"),
        P(None, "acct"),
        P(None, "acct", "rep", None),
        P(None, "rep", "acct"),
    ) + (P(),) * 9
    return jax.shard_map(
        per_device, mesh=mesh, in_specs=placed, out_specs=P("rep", "acct", None), check_vma=False
    )
```

```python
import functools

import jax
import jax.numpy as jnp
from jax import lax
from jax.experimental import pallas as pl
from jax.experimental.pallas import tpu as pltpu
from jax.sharding import PartitionSpec as P

NB = 3
NZ, NX, NC, NR = 8, 4, 2, 4
BD, TD, ROWS, D = 8, 32, 32, 512
PARTS = 1
PR = ROWS // PARTS
CAP = 2 * NZ * NC
DEPTHS = (15, 16, CAP)
COL = NZ * BD
BF, F32, I32 = jnp.bfloat16, jnp.float32, jnp.int32

SMEM = pl.BlockSpec(memory_space=pltpu.SMEM)
VMEM = pl.BlockSpec(memory_space=pltpu.VMEM)


def call(kernel, name, outs, specs, args, scratch=()):
    many = isinstance(outs, list)
    return pl.pallas_call(
        kernel,
        out_shape=outs,
        in_specs=specs,
        out_specs=[VMEM] * len(outs) if many else VMEM,
        scratch_shapes=scratch,
        compiler_params=pltpu.CompilerParams(vmem_limit_bytes=14 << 20),
        name=name,
    )(*args)


def shape(*dims, dtype=BF):
    return jax.ShapeDtypeStruct(dims, dtype)


def z_shift(s):
    n = NX * NC
    return [(i, ((i // n + s) % NZ) * n + i % n) for i in range(NZ * n)]


def x_shift(s):
    n = NX * NC
    return [(i, (i // n) * n + ((i // NC + s) % NX) * NC + i % NC) for i in range(NZ * n)]


def core_swap():
    return [(i, i ^ 1) for i in range(NZ * NX * NC)]


def rep_shift(s):
    return [(i, (i + s) % NR) for i in range(NR)]


def block_at(place, column, lanes):
    block = column[jnp.clip(place, 0, COL - 1)]
    for d, lane in enumerate(lanes):
        low = COL + d * CAP
        slot = jnp.clip(place - low, 0, lane.shape[0] - 1)
        block = jnp.where((place >= low) & (place < low + CAP), lane[slot], block)
    return block


def gather_kernel(batch, idx_ref, *refs):
    pieces, column, lanes = refs[:-NX], refs[-NX], refs[-NX + 1 :]
    low = 0
    for piece in pieces:
        column[low : low + piece.shape[0]] = piece[...]
        low += piece.shape[0]
    for s in range(lanes[0].shape[0]):
        for d, lane in enumerate(lanes):
            lane[s] = column[idx_ref[batch, d * CAP + s]]


def gather_call(batch, depth, idx, pieces):
    return call(
        functools.partial(gather_kernel, batch),
        "gather",
        [shape(COL, PR, D)] + [shape(depth, PR, D)] * (NX - 1),
        [SMEM] + [VMEM] * len(pieces),
        (idx, *pieces),
    )


def swap_kernel(batch, idx_ref, column, *refs):
    lanes, out = refs[:-1], refs[-1]
    for t in range(TD):
        out[t] = block_at(idx_ref[batch, t], column, lanes)


def swap_call(batch, idx, table):
    return call(
        functools.partial(swap_kernel, batch),
        "swap",
        shape(TD, PR, D),
        [SMEM] + [VMEM] * NX,
        (idx, *table),
    )


def hidden_of(block, code):
    return jnp.maximum(block.astype(F32) + code, 0.0).astype(BF)


def local_kernel(batch, idx_ref, code_ref, column, *refs):
    lanes, out = refs[:-1], refs[-1]
    for t in range(TD):
        block = block_at(idx_ref[batch, t], column, lanes)
        out[t] = hidden_of(block, code_ref[batch, t : t + 1, :])


def local_call(batch, idx, code, table):
    return call(
        functools.partial(local_kernel, batch),
        "local",
        shape(TD, PR, D),
        [SMEM] + [VMEM] * (1 + NX),
        (idx, code, *table),
    )


def message_kernel(batch, idx_ref, code_ref, w2_ref, local_ref, swapped_ref, out_ref, hidden_ref):
    for t in range(TD):
        crossed = hidden_of(swapped_ref[t], code_ref[batch, t : t + 1, :])
        hidden_ref[t] = jnp.where(idx_ref[batch, t] >= 0, local_ref[t], crossed)
    hidden = hidden_ref[...].reshape(TD * PR, D)
    out_ref[...] = jnp.dot(hidden, w2_ref[...], preferred_element_type=F32).astype(BF)


def message_call(batch, idx, code, w2, local, swapped):
    return call(
        functools.partial(message_kernel, batch),
        "message",
        shape(TD * PR, D),
        [SMEM] + [VMEM] * 4,
        (idx, code, w2, local, swapped),
        [pltpu.VMEM((TD, PR, D), BF)],
    )


def share_of(lhs_ref, messages, j):
    n, depth = BD * PR, TD * PR
    share = 0.0
    for p, message in enumerate(messages):
        lhs = lhs_ref[j * n : (j + 1) * n, p * depth : (p + 1) * depth]
        share = share + jnp.dot(lhs, message[...], preferred_element_type=F32)
    return share


def far_kernel(lhs_ref, *refs):
    messages, outs = refs[:PARTS], refs[PARTS:]
    half = BD * PR // 2
    share = share_of(lhs_ref, messages, 2).astype(BF)
    outs[0][...] = share[:half]
    outs[1][...] = share[half:]


def far_call(lhs, messages):
    half = BD * PR // 2
    return call(far_kernel, "far", [shape(half, D)] * 2, [VMEM] * (1 + PARTS), (lhs, *messages))


def near_kernel(lhs_ref, *refs):
    messages, outs = refs[:PARTS], refs[PARTS:]
    for j, out in zip((0, 1, 3), outs):
        out[...] = share_of(lhs_ref, messages, j)


def near_call(lhs, messages):
    n = BD * PR
    return call(near_kernel, "near", [shape(n, D, dtype=F32)] * 3, [VMEM] * (1 + PARTS), (lhs, *messages))


def fold_kernel(up_ref, down_ref, low_ref, high_ref, out_up, out_down):
    half = BD * PR // 2
    out_up[:half] = (up_ref[:half] + low_ref[...].astype(F32)).astype(BF)
    out_up[half:] = up_ref[half:].astype(BF)
    out_down[:half] = down_ref[:half].astype(BF)
    out_down[half:] = (down_ref[half:] + high_ref[...].astype(F32)).astype(BF)


def fold_call(*args):
    return call(fold_kernel, "fold", [shape(BD * PR, D)] * 2, [VMEM] * 4, args)


def over_rep(lhs, messages):
    low, high = far_call(lhs, messages)
    low = lax.ppermute(low, "rep", rep_shift(1))
    high = lax.ppermute(high, "rep", rep_shift(-1))
    own, up, down = near_call(lhs, messages)
    up, down = fold_call(up, down, low, high)
    return own, lax.ppermute(up, "rep", rep_shift(1)), lax.ppermute(down, "rep", rep_shift(-1))


def prepare_kernel(rep_ref, masks_ref, dst_ref, *outs):
    mask_ref = outs[-1]
    outs = outs[:-1]
    depth = TD * PR
    tile = lax.broadcasted_iota(I32, (TD, depth), 0)
    place = lax.broadcasted_iota(I32, (TD, depth), 1)
    spread = ((place >= tile * PR) & (place < (tile + 1) * PR)).astype(BF)
    block = lax.broadcasted_iota(I32, (BD, TD), 0)
    rep = rep_ref[0]
    for batch in range(NB):
        hot = (dst_ref[batch : batch + 1, :] == block).astype(BF)
        hot = jnp.dot(hot, spread, preferred_element_type=F32).astype(BF)
        for p in range(PARTS):
            bits = masks_ref[batch, :, p * PR : (p + 1) * PR, :].astype(F32)
            mask_ref[:, p * depth : (p + 1) * depth] = bits.reshape(depth, NR * ROWS).T.astype(BF)
        for j in range(NR):
            r = lax.rem(rep + j, NR)
            for q in range(PARTS):
                rows = mask_ref[pl.ds(pl.multiple_of(r * ROWS + q * PR, PR), PR), :]
                for k in range(BD):
                    low = (j * BD + k) * PR
                    for p in range(PARTS):
                        part = rows[:, p * depth : (p + 1) * depth]
                        outs[batch * PARTS + q][low : low + PR, p * depth : (p + 1) * depth] = part * hot[k : k + 1, :]


def prepare_call(rep, masks, dst):
    return call(
        prepare_kernel,
        "prepare",
        [shape(NR * BD * PR, TD * ROWS)] * (NB * PARTS),
        [SMEM] + [VMEM] * 2,
        (rep, masks, dst),
        [pltpu.VMEM((NR * ROWS, TD * ROWS), BF)],
    )


def sigmoid(v):
    return 0.5 * jnp.tanh(0.5 * v) + 0.5


def update_kernel(batch, part, last, own, in1, in2, state, member, gain, w_in, w_hid, b_in, b_hid, w1, *outs):
    total = own[...] + in1[...].astype(F32) + in2[...].astype(F32)
    mean = jnp.mean(total, axis=-1, keepdims=True)
    centred = total - mean
    var = jnp.mean(centred * centred, axis=-1, keepdims=True)
    x = (centred * lax.rsqrt(var + 1e-05) * gain[...]).astype(BF)
    old = state[...]
    gin = jnp.dot(x, w_in[...], preferred_element_type=F32) + b_in[...]
    ghid = jnp.dot(old, w_hid[...], preferred_element_type=F32) + b_hid[...]
    z = sigmoid(gin[:, :D] + ghid[:, :D])
    r = sigmoid(gin[:, D : 2 * D] + ghid[:, D : 2 * D])
    cand = jnp.tanh(gin[:, 2 * D :] + r * ghid[:, 2 * D :])
    fresh = (1.0 - z) * cand + z * old.astype(F32)
    new = jnp.where(member[batch, part] == 1, fresh, old.astype(F32)).astype(BF)
    outs[0][...] = new
    if not last:
        outs[1][...] = jnp.dot(new, w1[...], preferred_element_type=F32).astype(BF)


def update_call(batch, part, last, *args):
    return call(
        functools.partial(update_kernel, batch, part, last),
        "update",
        [shape(BD * PR, D)] * (1 if last else 2),
        [VMEM] * len(args),
        args,
    )


def first_kernel(state_ref, w1, *outs):
    for p in range(PARTS):
        state = state_ref[:, p * PR : (p + 1) * PR, :].reshape(BD * PR, D)
        outs[p][...] = jnp.dot(state, w1[...], preferred_element_type=F32).astype(BF)
        outs[PARTS + p][...] = state


def first_call(state, w1):
    return call(first_kernel, "first", [shape(BD * PR, D)] * (2 * PARTS), [VMEM] * 2, (state, w1))


def ranks(dev, loc):
    tile = jnp.arange(NC * TD, dtype=I32)
    before = tile[None, :] < tile[:, None]
    pair = dev % (NX * NC)
    lane = pair[..., :, None] == pair[..., None, :]
    block = dev * BD + loc
    same = block[..., :, None] == block[..., None, :]
    first = ~jnp.any(same & before, axis=-1)
    new = jnp.where(before & lane & first[..., None, :], 1, 0)
    rank = jnp.sum(new, axis=-1)
    home = jnp.sum(jnp.where(same & first[..., None, :], rank[..., None, :], 0), axis=-1)
    return home


def places(src_dev, src_local):
    me = lax.axis_index("acct")
    z, x, c = me // (NX * NC), (me // NC) % NX, me % NC
    dev = src_dev.reshape(NB, NZ, NX, NC * TD)
    loc = src_local.reshape(NB, NZ, NX, NC * TD)
    dev = lax.dynamic_slice_in_dim(dev, z, 1, 1)[:, 0]
    loc = lax.dynamic_slice_in_dim(loc, z, 1, 1)[:, 0]
    sz, sx, sc = dev // (NX * NC), (dev // NC) % NX, dev % NC
    column = ((sz - z) % NZ) * BD + loc
    rank = ranks(dev, loc)
    mine = sx * NC + sc == x * NC + c
    slots = jnp.arange(CAP, dtype=I32)
    chosen = mine[:, :, None, :] & (rank[:, :, None, :] == slots[None, None, :, None])
    out = jnp.max(jnp.where(chosen, column[:, :, None, :], 0), axis=-1)
    lanes = (x + jnp.arange(1, NX, dtype=I32)) % NX
    turn = (lanes[:, None] == jnp.arange(NX, dtype=I32)[None, :]).astype(I32)
    send = jnp.sum(out[:, None, :, :] * turn[None, :, :, None], axis=2).reshape(NB, -1)
    here = (jnp.arange(NX, dtype=I32) == x).astype(I32)[None, :, None]
    column, rank, sx, sc = (jnp.sum(a * here, axis=1) for a in (column, rank, sx, sc))
    lane = (sx - x) % NX
    place = jnp.where(lane == 0, column, COL + (lane - 1) * CAP + rank).reshape(NB, NC, TD)
    local = (sc == c).reshape(NB, NC, TD)
    self_ = (jnp.arange(NC, dtype=I32) == c).astype(I32)[None, :, None]
    final = jnp.sum(jnp.where(local, place, -1) * self_, axis=1)
    swap = jnp.sum(jnp.where(local, place, 0) * (1 - self_), axis=1)
    return send, swap, final


def deepest(src_dev, src_local):
    dev = src_dev.reshape(NZ, NX, NC * TD)
    loc = src_local.reshape(NZ, NX, NC * TD)
    away = (dev // NC) % NX != jnp.arange(NX, dtype=I32)[None, :, None]
    return jnp.max(jnp.where(away, ranks(dev, loc), 0)) + 1


def along_x(lanes):
    order = [2, 1, 3]
    got = {d: lax.ppermute(lanes[d - 1], "acct", x_shift(d)) for d in order}
    return [got[d] for d in range(NX - 1, 0, -1)]


def along_z(pre, beside=None):
    up, down, after = [pre], [pre], []
    for step in range(3):
        up.append(lax.ppermute(up[-1], "acct", z_shift(1)))
        down.append(lax.ppermute(down[-1], "acct", z_shift(-1)))
        if beside is not None:
            arrays, up[-1] = lax.optimization_barrier((beside[step], up[-1]))
            after.append(arrays)
    half = BD // 2
    far_up = lax.ppermute(up[3][:half], "acct", z_shift(1))
    far_down = lax.ppermute(down[3][half:], "acct", z_shift(-1))
    return [pre, down[1], down[2], down[3], far_up, far_down, up[3], up[2], up[1]], after


def per_device(
    memory, src_dev, src_local, dst_local, delta_t, masks, member,
    w_msg1, b_msg1, omega, w_msg2, ln_gain, w_in, w_hid, b_in, b_hid,
):
    rep = lax.axis_index("rep").reshape(1).astype(I32)
    first = first_call(jnp.swapaxes(memory, 0, 1), w_msg1)
    beside = [(src_dev[batch], src_local[batch]) for batch in range(NB)]
    columns = []
    for p in range(PARTS):
        column, after = along_z(first[p].reshape(BD, PR, D), beside)
        columns.append(column)
        beside = after
    send, swap, final = places(src_dev, src_local)
    depth = functools.reduce(jnp.maximum, [deepest(*arrays) for arrays in beside])
    branch = sum((depth > d).astype(I32) for d in DEPTHS[:-1])

    def run(depth, columns, state):
        code = jnp.cos(delta_t[:, :, None] * omega) + b_msg1
        lhs = prepare_call(rep, masks, dst_local)
        chosen = jnp.transpose(member.reshape(NB, PARTS, PR, BD), (0, 1, 3, 2)).reshape(NB, PARTS, BD * PR, 1)
        for batch in range(NB):
            last = batch == NB - 1
            messages = []
            for p in range(PARTS):
                column, *lanes = gather_call(batch, depth, send, columns[p])
                lanes = along_x(lanes)
                if batch == 0 and p == 0:
                    lanes, code, lhs, chosen = lax.optimization_barrier((lanes, code, lhs, chosen))
                table = [column, *lanes]
                swapped = lax.ppermute(swap_call(batch, swap, table), "acct", core_swap())
                local = local_call(batch, final, code, table)
                messages.append(message_call(batch, final, code, w_msg2, local, swapped))
            results = []
            for q in range(PARTS):
                shares = over_rep(lhs[batch * PARTS + q], messages)
                results.append(
                    update_call(
                        batch, q, last, *shares, state[q], chosen, ln_gain[None],
                        w_in, w_hid, b_in[None], b_hid[None], w_msg1,
                    )
                )
            state = [r[0] for r in results]
            if not last:
                columns = [along_z(r[1].reshape(BD, PR, D))[0] for r in results]
        return state

    branches = [functools.partial(run, depth) for depth in DEPTHS]
    state = lax.switch(branch, branches, columns, first[PARTS:])
    whole = jnp.concatenate([s.reshape(BD, PR, D) for s in state], axis=1)
    return jnp.swapaxes(whole, 0, 1)


def solution(mesh):
    placed = (
        P("rep", "acct", None),
        P(),
        P(),
        P(None, "acct"),
        P(None, "acct"),
        P(None, "acct", "rep", None),
        P(None, "rep", "acct"),
    ) + (P(),) * 9
    return jax.shard_map(
        per_device, mesh=mesh, in_specs=placed, out_specs=P("rep", "acct", None), check_vma=False
    )
```

```python
import functools

import jax
import jax.numpy as jnp
from jax import lax
from jax.experimental import pallas as pl
from jax.experimental.pallas import tpu as pltpu
from jax.sharding import PartitionSpec as P

NB = 3
NZ, NX, NC, NR = 8, 4, 2, 4
BD, TD, ROWS, D = 8, 32, 32, 512
PARTS = 1
PR = ROWS // PARTS
CAP = 2 * NZ * NC
DEPTHS = (15, 16, CAP)
COL = NZ * BD
BF, F32, I32 = jnp.bfloat16, jnp.float32, jnp.int32

SMEM = pl.BlockSpec(memory_space=pltpu.SMEM)
VMEM = pl.BlockSpec(memory_space=pltpu.VMEM)


def call(kernel, name, outs, specs, args, scratch=()):
    many = isinstance(outs, list)
    return pl.pallas_call(
        kernel,
        out_shape=outs,
        in_specs=specs,
        out_specs=[VMEM] * len(outs) if many else VMEM,
        scratch_shapes=scratch,
        compiler_params=pltpu.CompilerParams(vmem_limit_bytes=14 << 20),
        name=name,
    )(*args)


def shape(*dims, dtype=BF):
    return jax.ShapeDtypeStruct(dims, dtype)


def z_shift(s):
    n = NX * NC
    return [(i, ((i // n + s) % NZ) * n + i % n) for i in range(NZ * n)]


def x_shift(s):
    n = NX * NC
    return [(i, (i // n) * n + ((i // NC + s) % NX) * NC + i % NC) for i in range(NZ * n)]


def core_swap():
    return [(i, i ^ 1) for i in range(NZ * NX * NC)]


def rep_shift(s):
    return [(i, (i + s) % NR) for i in range(NR)]


def block_at(place, column, lanes):
    block = column[jnp.clip(place, 0, COL - 1)]
    for d, lane in enumerate(lanes):
        low = COL + d * CAP
        slot = jnp.clip(place - low, 0, lane.shape[0] - 1)
        block = jnp.where((place >= low) & (place < low + CAP), lane[slot], block)
    return block


def gather_kernel(batch, idx_ref, *refs):
    pieces, column, lanes = refs[:-NX], refs[-NX], refs[-NX + 1 :]
    low = 0
    for piece in pieces:
        column[low : low + piece.shape[0]] = piece[...]
        low += piece.shape[0]
    for s in range(lanes[0].shape[0]):
        for d, lane in enumerate(lanes):
            lane[s] = column[idx_ref[batch, d * CAP + s]]


def gather_call(batch, depth, idx, pieces):
    return call(
        functools.partial(gather_kernel, batch),
        "gather",
        [shape(COL, PR, D)] + [shape(depth, PR, D)] * (NX - 1),
        [SMEM] + [VMEM] * len(pieces),
        (idx, *pieces),
    )


def swap_kernel(batch, idx_ref, column, *refs):
    lanes, out = refs[:-1], refs[-1]
    for t in range(TD):
        out[t] = block_at(idx_ref[batch, t], column, lanes)


def swap_call(batch, idx, table):
    return call(
        functools.partial(swap_kernel, batch),
        "swap",
        shape(TD, PR, D),
        [SMEM] + [VMEM] * NX,
        (idx, *table),
    )


def hidden_of(block, code):
    return jnp.maximum(block.astype(F32) + code, 0.0).astype(BF)


def local_kernel(batch, idx_ref, code_ref, column, *refs):
    lanes, out = refs[:-1], refs[-1]
    for t in range(TD):
        block = block_at(idx_ref[batch, t], column, lanes)
        out[t] = hidden_of(block, code_ref[batch, t : t + 1, :])


def local_call(batch, idx, code, table):
    return call(
        functools.partial(local_kernel, batch),
        "local",
        shape(TD, PR, D),
        [SMEM] + [VMEM] * (1 + NX),
        (idx, code, *table),
    )


def message_kernel(batch, idx_ref, code_ref, w2_ref, local_ref, swapped_ref, out_ref, hidden_ref):
    for t in range(TD):
        crossed = hidden_of(swapped_ref[t], code_ref[batch, t : t + 1, :])
        hidden_ref[t] = jnp.where(idx_ref[batch, t] >= 0, local_ref[t], crossed)
    hidden = hidden_ref[...].reshape(TD * PR, D)
    out_ref[...] = jnp.dot(hidden, w2_ref[...], preferred_element_type=F32).astype(BF)


def message_call(batch, idx, code, w2, local, swapped):
    return call(
        functools.partial(message_kernel, batch),
        "message",
        shape(TD * PR, D),
        [SMEM] + [VMEM] * 4,
        (idx, code, w2, local, swapped),
        [pltpu.VMEM((TD, PR, D), BF)],
    )


def share_of(lhs_ref, messages, j):
    n, depth = BD * PR, TD * PR
    share = 0.0
    for p, message in enumerate(messages):
        lhs = lhs_ref[j * n : (j + 1) * n, p * depth : (p + 1) * depth]
        share = share + jnp.dot(lhs, message[...], preferred_element_type=F32)
    return share


def far_kernel(lhs_ref, *refs):
    messages, outs = refs[:PARTS], refs[PARTS:]
    half = BD * PR // 2
    share = share_of(lhs_ref, messages, 2).astype(BF)
    outs[0][...] = share[:half]
    outs[1][...] = share[half:]


def far_call(lhs, messages):
    half = BD * PR // 2
    return call(far_kernel, "far", [shape(half, D)] * 2, [VMEM] * (1 + PARTS), (lhs, *messages))


def near_kernel(lhs_ref, *refs):
    messages, outs = refs[:PARTS], refs[PARTS:]
    for j, out in zip((0, 1, 3), outs):
        out[...] = share_of(lhs_ref, messages, j)


def near_call(lhs, messages):
    n = BD * PR
    return call(near_kernel, "near", [shape(n, D, dtype=F32)] * 3, [VMEM] * (1 + PARTS), (lhs, *messages))


def fold_kernel(up_ref, down_ref, low_ref, high_ref, out_up, out_down):
    half = BD * PR // 2
    out_up[:half] = (up_ref[:half] + low_ref[...].astype(F32)).astype(BF)
    out_up[half:] = up_ref[half:].astype(BF)
    out_down[:half] = down_ref[:half].astype(BF)
    out_down[half:] = (down_ref[half:] + high_ref[...].astype(F32)).astype(BF)


def fold_call(*args):
    return call(fold_kernel, "fold", [shape(BD * PR, D)] * 2, [VMEM] * 4, args)


def over_rep(lhs, messages):
    low, high = far_call(lhs, messages)
    low = lax.ppermute(low, "rep", rep_shift(1))
    high = lax.ppermute(high, "rep", rep_shift(-1))
    own, up, down = near_call(lhs, messages)
    up, down = fold_call(up, down, low, high)
    return own, lax.ppermute(up, "rep", rep_shift(1)), lax.ppermute(down, "rep", rep_shift(-1))


def prepare_kernel(batch, rep_ref, masks_ref, dst_ref, *outs):
    mask_ref = outs[-1]
    outs = outs[:-1]
    depth = TD * PR
    tile = lax.broadcasted_iota(I32, (TD, depth), 0)
    place = lax.broadcasted_iota(I32, (TD, depth), 1)
    spread = ((place >= tile * PR) & (place < (tile + 1) * PR)).astype(BF)
    block = lax.broadcasted_iota(I32, (BD, TD), 0)
    rep = rep_ref[0]
    hot = (dst_ref[batch : batch + 1, :] == block).astype(BF)
    hot = jnp.dot(hot, spread, preferred_element_type=F32).astype(BF)
    for p in range(PARTS):
        bits = masks_ref[batch, :, p * PR : (p + 1) * PR, :].astype(F32)
        mask_ref[:, p * depth : (p + 1) * depth] = bits.reshape(depth, NR * ROWS).T.astype(BF)
    for j in range(NR):
        r = lax.rem(rep + j, NR)
        for q in range(PARTS):
            rows = mask_ref[pl.ds(pl.multiple_of(r * ROWS + q * PR, PR), PR), :]
            for k in range(BD):
                low = (j * BD + k) * PR
                for p in range(PARTS):
                    part = rows[:, p * depth : (p + 1) * depth]
                    outs[q][low : low + PR, p * depth : (p + 1) * depth] = part * hot[k : k + 1, :]


def prepare_call(batch, rep, masks, dst):
    return call(
        functools.partial(prepare_kernel, batch),
        "prepare",
        [shape(NR * BD * PR, TD * ROWS)] * PARTS,
        [SMEM] + [VMEM] * 2,
        (rep, masks, dst),
        [pltpu.VMEM((NR * ROWS, TD * ROWS), BF)],
    )


def sigmoid(v):
    return 0.5 * jnp.tanh(0.5 * v) + 0.5


def update_kernel(batch, part, last, own, in1, in2, state, member, gain, w_in, w_hid, b_in, b_hid, w1, *outs):
    total = own[...] + in1[...].astype(F32) + in2[...].astype(F32)
    mean = jnp.mean(total, axis=-1, keepdims=True)
    centred = total - mean
    var = jnp.mean(centred * centred, axis=-1, keepdims=True)
    x = (centred * lax.rsqrt(var + 1e-05) * gain[...]).astype(BF)
    old = state[...]
    gin = jnp.dot(x, w_in[...], preferred_element_type=F32) + b_in[...]
    ghid = jnp.dot(old, w_hid[...], preferred_element_type=F32) + b_hid[...]
    z = sigmoid(gin[:, :D] + ghid[:, :D])
    r = sigmoid(gin[:, D : 2 * D] + ghid[:, D : 2 * D])
    cand = jnp.tanh(gin[:, 2 * D :] + r * ghid[:, 2 * D :])
    fresh = (1.0 - z) * cand + z * old.astype(F32)
    new = jnp.where(member[batch, part] == 1, fresh, old.astype(F32)).astype(BF)
    outs[0][...] = new
    if not last:
        outs[1][...] = jnp.dot(new, w1[...], preferred_element_type=F32).astype(BF)


def update_call(batch, part, last, *args):
    return call(
        functools.partial(update_kernel, batch, part, last),
        "update",
        [shape(BD * PR, D)] * (1 if last else 2),
        [VMEM] * len(args),
        args,
    )


def first_kernel(state_ref, w1, *outs):
    for p in range(PARTS):
        state = state_ref[:, p * PR : (p + 1) * PR, :].reshape(BD * PR, D)
        outs[p][...] = jnp.dot(state, w1[...], preferred_element_type=F32).astype(BF)
        outs[PARTS + p][...] = state


def first_call(state, w1):
    return call(first_kernel, "first", [shape(BD * PR, D)] * (2 * PARTS), [VMEM] * 2, (state, w1))


def ranks(dev, loc):
    tile = jnp.arange(NC * TD, dtype=I32)
    before = tile[None, :] < tile[:, None]
    pair = dev % (NX * NC)
    lane = pair[..., :, None] == pair[..., None, :]
    block = dev * BD + loc
    same = block[..., :, None] == block[..., None, :]
    first = ~jnp.any(same & before, axis=-1)
    new = jnp.where(before & lane & first[..., None, :], 1, 0)
    rank = jnp.sum(new, axis=-1)
    home = jnp.sum(jnp.where(same & first[..., None, :], rank[..., None, :], 0), axis=-1)
    return home


def places(src_dev, src_local):
    me = lax.axis_index("acct")
    z, x, c = me // (NX * NC), (me // NC) % NX, me % NC
    dev = src_dev.reshape(NB, NZ, NX, NC * TD)
    loc = src_local.reshape(NB, NZ, NX, NC * TD)
    dev = lax.dynamic_slice_in_dim(dev, z, 1, 1)[:, 0]
    loc = lax.dynamic_slice_in_dim(loc, z, 1, 1)[:, 0]
    sz, sx, sc = dev // (NX * NC), (dev // NC) % NX, dev % NC
    column = ((sz - z) % NZ) * BD + loc
    rank = ranks(dev, loc)
    mine = sx * NC + sc == x * NC + c
    slots = jnp.arange(CAP, dtype=I32)
    chosen = mine[:, :, None, :] & (rank[:, :, None, :] == slots[None, None, :, None])
    out = jnp.max(jnp.where(chosen, column[:, :, None, :], 0), axis=-1)
    lanes = (x + jnp.arange(1, NX, dtype=I32)) % NX
    turn = (lanes[:, None] == jnp.arange(NX, dtype=I32)[None, :]).astype(I32)
    send = jnp.sum(out[:, None, :, :] * turn[None, :, :, None], axis=2).reshape(NB, -1)
    here = (jnp.arange(NX, dtype=I32) == x).astype(I32)[None, :, None]
    column, rank, sx, sc = (jnp.sum(a * here, axis=1) for a in (column, rank, sx, sc))
    lane = (sx - x) % NX
    place = jnp.where(lane == 0, column, COL + (lane - 1) * CAP + rank).reshape(NB, NC, TD)
    local = (sc == c).reshape(NB, NC, TD)
    self_ = (jnp.arange(NC, dtype=I32) == c).astype(I32)[None, :, None]
    final = jnp.sum(jnp.where(local, place, -1) * self_, axis=1)
    swap = jnp.sum(jnp.where(local, place, 0) * (1 - self_), axis=1)
    return send, swap, final


def deepest(src_dev, src_local):
    dev = src_dev.reshape(NB, NZ, NX, NC * TD)
    loc = src_local.reshape(NB, NZ, NX, NC * TD)
    away = (dev // NC) % NX != jnp.arange(NX, dtype=I32)[None, None, :, None]
    return jnp.max(jnp.where(away, ranks(dev, loc), 0)) + 1


def along_x(lanes):
    order = [2, 1, 3]
    got = {d: lax.ppermute(lanes[d - 1], "acct", x_shift(d)) for d in order}
    return [got[d] for d in range(NX - 1, 0, -1)]


def along_z(pre, beside=None):
    up, down = [pre], [pre]
    for step in range(3):
        up.append(lax.ppermute(up[-1], "acct", z_shift(1)))
        down.append(lax.ppermute(down[-1], "acct", z_shift(-1)))
        if beside is not None and step == 0:
            beside, up[-1] = lax.optimization_barrier((beside, up[-1]))
    half = BD // 2
    far_up = lax.ppermute(up[3][:half], "acct", z_shift(1))
    far_down = lax.ppermute(down[3][half:], "acct", z_shift(-1))
    return [pre, down[1], down[2], down[3], far_up, far_down, up[3], up[2], up[1]], beside


def per_device(
    memory, src_dev, src_local, dst_local, delta_t, masks, member,
    w_msg1, b_msg1, omega, w_msg2, ln_gain, w_in, w_hid, b_in, b_hid,
):
    rep = lax.axis_index("rep").reshape(1).astype(I32)
    first = first_call(jnp.swapaxes(memory, 0, 1), w_msg1)
    beside = (src_dev, src_local)
    columns = []
    for p in range(PARTS):
        column, beside = along_z(first[p].reshape(BD, PR, D), beside)
        columns.append(column)
    send, swap, final = places(src_dev, src_local)
    depth = deepest(*beside)
    branch = sum((depth > d).astype(I32) for d in DEPTHS[:-1])

    def run(depth, columns, state):
        code = jnp.cos(delta_t[:, :, None] * omega) + b_msg1
        chosen = jnp.transpose(member.reshape(NB, PARTS, PR, BD), (0, 1, 3, 2)).reshape(NB, PARTS, BD * PR, 1)
        for batch in range(NB):
            last = batch == NB - 1
            messages = []
            for p in range(PARTS):
                column, *lanes = gather_call(batch, depth, send, columns[p])
                if p == 0:
                    bits, lanes[0] = lax.optimization_barrier((masks, lanes[0]))
                    lhs = prepare_call(batch, rep, bits, dst_local)
                lanes = along_x(lanes)
                if p == 0:
                    lanes, code, lhs, chosen = lax.optimization_barrier((lanes, code, lhs, chosen))
                table = [column, *lanes]
                swapped = lax.ppermute(swap_call(batch, swap, table), "acct", core_swap())
                local = local_call(batch, final, code, table)
                messages.append(message_call(batch, final, code, w_msg2, local, swapped))
            results = []
            for q in range(PARTS):
                shares = over_rep(lhs[q], messages)
                results.append(
                    update_call(
                        batch, q, last, *shares, state[q], chosen, ln_gain[None],
                        w_in, w_hid, b_in[None], b_hid[None], w_msg1,
                    )
                )
            state = [r[0] for r in results]
            if not last:
                columns = [along_z(r[1].reshape(BD, PR, D))[0] for r in results]
        return state

    branches = [functools.partial(run, depth) for depth in DEPTHS]
    state = lax.switch(branch, branches, columns, first[PARTS:])
    whole = jnp.concatenate([s.reshape(BD, PR, D) for s in state], axis=1)
    return jnp.swapaxes(whole, 0, 1)


def solution(mesh):
    placed = (
        P("rep", "acct", None),
        P(),
        P(),
        P(None, "acct"),
        P(None, "acct"),
        P(None, "acct", "rep", None),
        P(None, "rep", "acct"),
    ) + (P(),) * 9
    return jax.shard_map(
        per_device, mesh=mesh, in_specs=placed, out_specs=P("rep", "acct", None), check_vma=False
    )
```
